128 devices in a mesh: ctx: 16 (over x, z), tp: 8 (over y, core).
Axes of the slice: x: 4, y: 4, z: 4, core: 2. Of those that a mesh axis runs over, the one named last changes fastest.
Arguments:
- queries: bfloat16 [16384, 256], P('ctx', 'tp'), may hold values from -6 to 6
- keys: bfloat16 [16384, 256], P('ctx', 'tp'), may hold values from -6 to 6
- values: bfloat16 [16384, 4096], P('ctx', 'tp'), may hold values from -6 to 6
- conv_weight: float32 [3, 4096], P(None, 'tp'), may hold values from -3 to 3
- w_out: bfloat16 [4096, 4096], P(None, 'tp'), may hold values from -0.375 to 0.375
- cotangent: bfloat16 [16384, 4096], P('ctx', 'tp'), may hold values from -6 to 6
Outputs:
- layer_out: bfloat16 [16384, 4096], P('ctx', 'tp')
- grad_queries: bfloat16 [16384, 256], P('ctx', 'tp')
- grad_keys: bfloat16 [16384, 256], P('ctx', 'tp')
- grad_values: bfloat16 [16384, 4096], P('ctx', 'tp')
- grad_w_out: float32 [4096, 4096], P('ctx', 'tp')
The draws below stay inside these ranges and needn't reach their ends.
All inputs are finite; a program needn't handle non-finite values.
Results may differ from the reference program's by a relative error of at most 0.015.
Values may be sent and summed in bfloat16 or wider, within the bound.
A program may use at most 192 MiB of HBM per device.

```python
import math
import jax
import jax.numpy as jnp
from jax import lax

D = 4096
H = 16
FEAT = 16
DV = 256
KC = 3
TOK_DEV = 1024
FT = 273
HL = 2
TOKENS = 16384
N_TP = 8


def with_spikes(values, rng, source, target, shards_of, factor):
    def block_of(dim):
        return (jnp.arange(values.shape[dim]) // (values.shape[dim] // shards_of)).reshape((-1,) + (1,) * (values.ndim - 1 - dim))

    first = jax.random.permutation(rng, shards_of)[block_of(target)]
    far = (block_of(target) + shards_of // 2) % shards_of
    return jnp.where((block_of(source) == first) | (block_of(source) == far), factor * values, values)


def steps_of(stream_key, extent, shards, smallest, high):
    factor_of = 1.0
    for dim, blocks in shards:
        heights = jax.random.uniform(jax.random.fold_in(jax.random.fold_in(stream_key, 6), dim), (blocks,), jnp.float32, smallest / len(shards), high / len(shards))
        factor_of = factor_of * jnp.repeat(jnp.exp(heights), extent[dim] // blocks).reshape((-1,) + (1,) * (len(extent) - 1 - dim))
    return factor_of


def centred(rng, shape, width, limit, shards=(), dtype=jnp.bfloat16):
    gain = steps_of(rng, shape, shards, -0.22, 0.18) if shards else 1.0
    values = jax.random.normal(rng, shape, jnp.float32) * width * gain
    return jnp.minimum(jnp.maximum(values, -limit), limit).astype(dtype)


def bell_draw_with(rng, extent, deviation, bound, cuts, heavy, held_as=jnp.bfloat16):
    result = deviation * jax.random.normal(rng, extent, jnp.float32)
    if cuts:
        result = result * steps_of(rng, extent, cuts, -0.22, 0.18)
    return jnp.clip(with_spikes(result, jax.random.fold_in(rng, 3), *heavy), -bound, bound).astype(held_as)


def setup_inputs(seed: int = 0) -> dict:
    key_list = jax.random.split(jax.random.key(seed), 7)
    return {
        "queries": centred(key_list[0], (TOKENS, H * FEAT), 1.0, 6.0, ((0, 16), (1, 8))),
        "keys": centred(key_list[1], (TOKENS, H * FEAT), 1.0, 6.0, ((0, 16), (1, 8))),
        "values": centred(key_list[2], (TOKENS, H * DV), 1.0, 6.0, ((0, 16), (1, 8))),
        "conv_weight": centred(key_list[3], (KC, H * DV), 0.6, 3.0, ((1, 8),), jnp.float32),
        "w_out": centred(key_list[4], (D, H * DV), DV ** -0.5, 0.375, ((1, 8),)),
        "cotangent": bell_draw_with(key_list[5], (TOKENS, D), 1.0, 6.0, ((0, 16), (1, 8)), (0, 1, 16, 2.0)),
    }


PRECISE = lax.Precision.HIGHEST

def feature_map(vector):
    feat_dim = vector.shape[-1]
    sqrt_feat = math.sqrt(feat_dim)
    square_part = (vector[..., :, None] * vector[..., None, :]).reshape(vector.shape[:-1] + (feat_dim * feat_dim,))
    unit_col = jnp.ones(vector.shape[:-1] + (1,), jnp.float32)
    return jnp.concatenate([unit_col, vector / math.sqrt(sqrt_feat), square_part / (math.sqrt(2.0) * sqrt_feat)], axis=-1)

def feature_grad(vector, grad_feat):
    feat_dim = vector.shape[-1]
    sqrt_feat = math.sqrt(feat_dim)
    linear = grad_feat[..., 1:1 + feat_dim] / math.sqrt(sqrt_feat)
    square = grad_feat[..., 1 + feat_dim:].reshape(grad_feat.shape[:-1] + (feat_dim, feat_dim))
    symmetric = square + jnp.swapaxes(square, -1, -2)
    return linear + jnp.einsum('...ij,...j->...i', symmetric, vector, precision=PRECISE) / (math.sqrt(2.0) * sqrt_feat)

def to_blocks(array, block_rows):
    return array.reshape((array.shape[0] // block_rows, block_rows) + array.shape[1:])

def reference(queries, keys, values, conv_weight, w_out, cotangent):
    tok_rows = values.shape[0]
    taps_count = conv_weight.shape[0]
    block_rows = min(TOK_DEV, 256)
    padded = jnp.pad(values.astype(jnp.float32), ((taps_count - 1, 0), (0, 0)))
    conv_sum = jnp.zeros((tok_rows, values.shape[1]), jnp.float32)
    for tap_index in range(taps_count):
        conv_sum = conv_sum + conv_weight[tap_index] * padded[taps_count - 1 - tap_index:taps_count - 1 - tap_index + tok_rows]
    mixed_values = lax.optimization_barrier(conv_sum.astype(jnp.bfloat16))
    q_in = queries.astype(jnp.float32).reshape(tok_rows, H, FEAT)
    k_in = keys.astype(jnp.float32).reshape(tok_rows, H, FEAT)
    q_feat = lax.optimization_barrier(feature_map(q_in).astype(jnp.bfloat16))
    k_feat = lax.optimization_barrier(feature_map(k_in).astype(jnp.bfloat16))
    q_blocks = to_blocks(q_feat.astype(jnp.float32), block_rows)
    k_blocks = to_blocks(k_feat.astype(jnp.float32), block_rows)
    u_blocks = to_blocks(mixed_values.astype(jnp.float32).reshape(tok_rows, H, DV), block_rows)
    causal = jnp.tril(jnp.ones((block_rows, block_rows), jnp.bool_))

    def forward_step(running, block_data):
        state_sum, norm_sum = running
        q_part, k_part, u_part = block_data
        scores = jnp.where(causal, jnp.einsum('thf,shf->hts', q_part, k_part, precision=PRECISE), 0.0)
        numerator = jnp.einsum('hts,shv->thv', scores, u_part, precision=PRECISE) + jnp.einsum('thf,hfv->thv', q_part, state_sum, precision=PRECISE)
        denominator = lax.optimization_barrier(jnp.sum(scores, axis=2)).T + jnp.einsum('thf,hf->th', q_part, norm_sum, precision=PRECISE)
        updated = (state_sum + jnp.einsum('shf,shv->hfv', k_part, u_part, precision=PRECISE), norm_sum + lax.optimization_barrier(jnp.sum(k_part, axis=0)))
        return (updated, (numerator, denominator, state_sum, norm_sum))
    start_sums = (jnp.zeros((H, FT, DV), jnp.float32), jnp.zeros((H, FT), jnp.float32))
    _, (numerator, denominator, state_before, norm_before) = lax.scan(forward_step, start_sums, (q_blocks, k_blocks, u_blocks))
    attended = (numerator / denominator[..., None]).reshape(tok_rows, H * DV).astype(jnp.bfloat16)
    layer_out = jnp.zeros((tok_rows, D), jnp.float32)
    group_cols = HL * DV
    for group in range(N_TP):
        partial_g = jnp.dot(attended[:, group * group_cols:(group + 1) * group_cols], w_out[:, group * group_cols:(group + 1) * group_cols].T, preferred_element_type=jnp.float32).astype(jnp.bfloat16)
        layer_out = layer_out + lax.optimization_barrier(partial_g).astype(jnp.float32)
    layer_out = layer_out.astype(jnp.bfloat16)
    grad_attended = lax.optimization_barrier(jnp.dot(cotangent, w_out, preferred_element_type=jnp.float32).astype(jnp.bfloat16))
    grad_w_out = lax.dot_general(cotangent, attended, (((0,), (0,)), ((), ())), preferred_element_type=jnp.float32)
    g_blocks = to_blocks(grad_attended.astype(jnp.float32).reshape(tok_rows, H, DV), block_rows)

    def backward_step(running, block_data):
        grad_state, grad_norm = running
        q_part, k_part, u_part, g_part, numer_part, denom_part, state_part, norm_part = block_data
        grad_numer = g_part / denom_part[..., None]
        grad_denom = -lax.optimization_barrier(jnp.sum(g_part * numer_part, axis=-1)) / (denom_part * denom_part)
        scores = jnp.where(causal, jnp.einsum('thf,shf->hts', q_part, k_part, precision=PRECISE), 0.0)
        weights_grad = jnp.where(causal, jnp.einsum('thv,shv->hts', grad_numer, u_part, precision=PRECISE) + grad_denom.T[:, :, None], 0.0)
        grad_qfeat = jnp.einsum('hts,shf->thf', weights_grad, k_part, precision=PRECISE) + jnp.einsum('thv,hfv->thf', grad_numer, state_part, precision=PRECISE) + grad_denom[..., None] * norm_part[None]
        grad_kfeat = jnp.einsum('hts,thf->shf', weights_grad, q_part, precision=PRECISE) + jnp.einsum('shv,hfv->shf', u_part, grad_state, precision=PRECISE) + grad_norm[None]
        grad_mixed = jnp.einsum('hts,thv->shv', scores, grad_numer, precision=PRECISE) + jnp.einsum('shf,hfv->shv', k_part, grad_state, precision=PRECISE)
        updated = (grad_state + jnp.einsum('thf,thv->hfv', q_part, grad_numer, precision=PRECISE), grad_norm + jnp.einsum('thf,th->hf', q_part, grad_denom, precision=PRECISE))
        return (updated, (grad_qfeat, grad_kfeat, grad_mixed))
    _, (grad_qfeat, grad_kfeat, grad_mixed) = lax.scan(backward_step, start_sums, (q_blocks, k_blocks, u_blocks, g_blocks, numerator, denominator, state_before, norm_before), reverse=True)
    grad_queries = feature_grad(q_in, grad_qfeat.reshape(tok_rows, H, FT)).reshape(tok_rows, H * FEAT).astype(jnp.bfloat16)
    grad_keys = feature_grad(k_in, grad_kfeat.reshape(tok_rows, H, FT)).reshape(tok_rows, H * FEAT).astype(jnp.bfloat16)
    grad_flat = grad_mixed.reshape(tok_rows, H * DV)
    padded_grad = jnp.pad(grad_flat, ((0, taps_count - 1), (0, 0)))
    grad_values = jnp.zeros((tok_rows, H * DV), jnp.float32)
    for tap_index in range(taps_count):
        grad_values = grad_values + conv_weight[tap_index] * padded_grad[tap_index:tap_index + tok_rows]
    return (layer_out, grad_queries, grad_keys, grad_values.astype(jnp.bfloat16), grad_w_out)
```

```python
import functools
import math

import jax
import jax.numpy as jnp
import numpy as np
from jax import lax
from jax.experimental import pallas as pl
from jax.experimental.pallas import tpu as pltpu
from jax.sharding import PartitionSpec as P

MESH = pl.DeviceIdType.MESH
F32 = jnp.float32
BF16 = jnp.bfloat16

FEAT = 16
HL = 2
DV = 256
COLS = HL * DV
TOK = 1024
D = 4096
CH = 256
NC = TOK // CH
HALF = TOK // 2
FW = 256
FR = 160
SR = FR + 16


def nn(a, b):
    return lax.dot_general(a, b, (((1,), (0,)), ((), ())), preferred_element_type=F32)


def nt(a, b):
    return lax.dot_general(a, b, (((1,), (1,)), ((), ())), preferred_element_type=F32)


def tn(a, b):
    return lax.dot_general(a, b, (((0,), (0,)), ((), ())), preferred_element_type=F32)


def feature_tables():
    pairs = [(FEAT, FEAT, 1.0)]
    pairs += [(i, FEAT, 1.0 / math.sqrt(math.sqrt(FEAT))) for i in range(FEAT)]
    for i in range(FEAT):
        for j in range(i, FEAT):
            scale = 1.0 / (math.sqrt(2.0) * math.sqrt(FEAT))
            pairs.append((i, j, scale if i == j else scale * math.sqrt(2.0)))
    first = np.zeros((HL * FEAT, HL * FW), np.float32)
    second = np.zeros((HL * FEAT, HL * FW), np.float32)
    rows = np.zeros((8, HL * FW), np.float32)
    for h in range(HL):
        for col, (i, j, scale) in enumerate(pairs):
            at = h * FW + col
            if i == FEAT:
                rows[0, at] = 1.0
            else:
                first[h * FEAT + i, at] = 1.0
            if j == FEAT:
                rows[1, at] = 1.0
            else:
                second[h * FEAT + j, at] = 1.0
            rows[2, at] = scale
    return first, second, rows


def kernel(
    q_ref, k_ref, cw_ref, ra_ref, rb_ref, rows_ref, val_hbm, w_hbm, cot_hbm,
    out_ref, gq_ref, gk_ref, gv_ref, gw_ref,
    cfull, w, wx, vext, u, qf, kf, num, den, gd, att, attp, att_t, ga, gab, gm, gks,
    sc, sb, gb, zc, zb, gzc, gzb,
    f_send, f_line, f_tot, f_tots, f_back, f_prior,
    b_send, b_line, b_tot, b_tots, b_back, b_prior,
    so, rhalf, rfull, gs, ghalf, gfull, ph, hs, hhalf, hfull,
    send_sems, recv_sems, local_sems,
):
    ctx = lax.axis_index("ctx")
    tp = lax.axis_index("tp")
    x, z = ctx // 4, ctx % 4
    y, c = tp // 2, tp % 2
    yr, yl, yo = (y + 1) % 4, (y + 3) % 4, (y + 2) % 4
    partner = {"ctx": ctx, "tp": y * 2 + (1 - c)}
    to_right = {"ctx": ctx, "tp": yr * 2 + c}
    to_left = {"ctx": ctx, "tp": yl * 2 + c}
    later = {"ctx": (ctx + 1) % 16, "tp": tp}
    earlier = {"ctx": (ctx + 15) % 16, "tp": tp}
    zs = [{"ctx": x * 4 + (z + d) % 4, "tp": tp} for d in range(4)]
    xs = [{"ctx": ((x + d) % 4) * 4 + z, "tp": tp} for d in range(4)]

    names = {}
    pending = []

    def number(name):
        return names.setdefault(name, len(names))

    def remote(src, dst, name, dev):
        i = number(name)
        return pltpu.make_async_remote_copy(
            src_ref=src, dst_ref=dst, send_sem=send_sems.at[i], recv_sem=recv_sems.at[i],
            device_id=dev, device_id_type=MESH,
        )

    def send(src, dst, name, dev):
        copy = remote(src, dst, name, dev)
        copy.start()
        pending.append(copy)

    def arrived(dst, name):
        remote(dst, dst, name, partner).wait_recv()

    own_w = pltpu.make_async_copy(w_hbm, w, local_sems.at[0])
    own_v = pltpu.make_async_copy(val_hbm, vext.at[pl.ds(16, TOK)], local_sems.at[1])
    own_c = pltpu.make_async_copy(cot_hbm, cfull.at[tp], local_sems.at[2])
    own_v.start()
    own_c.start()
    own_w.start()

    barrier = pltpu.get_barrier_semaphore()
    peers = [partner, to_right, to_left, later, earlier] + zs[1:] + xs[1:]
    for peer in peers:
        pl.semaphore_signal(barrier, inc=1, device_id=peer, device_id_type=MESH)
    pl.semaphore_wait(barrier, len(peers))

    first, second = pl.ds(0, HALF), pl.ds(HALF, HALF)
    mine, from_r, from_l, from_o = tp, yr * 2 + c, yl * 2 + c, yo * 2 + c
    send(val_hbm.at[pl.ds(TOK - 16, 16)], vext.at[pl.ds(0, 16)], "halo", later)
    send(cot_hbm.at[first], cfull.at[mine, first], "r0", to_right)
    send(cot_hbm.at[second], cfull.at[mine, second], "l1", to_left)
    send(cot_hbm.at[second], cfull.at[mine, second], "r1", to_right)
    send(cot_hbm.at[first], cfull.at[mine, first], "l0", to_left)
    send(cot_hbm, cfull.at[mine], "p", partner)
    for yy in range(4):
        rows = pl.ds(pl.multiple_of((yy * 2 + 1 - c) * COLS, COLS), COLS)
        send(w_hbm.at[rows], wx.at[yy], ("w", yy), partner)

    def span(i, size=CH):
        return pl.ds(pl.multiple_of(i * size, size), size)

    lane = lax.broadcasted_iota(jnp.int32, (CH, HL * FEAT), 1)
    row_id = lax.broadcasted_iota(jnp.int32, (CH, COLS), 0)
    causal = lax.broadcasted_iota(jnp.int32, (CH, CH), 0) >= lax.broadcasted_iota(jnp.int32, (CH, CH), 1)

    def head_of(value, h):
        return jnp.where(lane // FEAT == h, value, jnp.zeros_like(value))

    def factors(value):
        return nn(value, ra_ref[...]) + rows_ref[0:1], nn(value, rb_ref[...]) + rows_ref[1:2]

    def features(value):
        a, b = factors(value)
        return (a * b * rows_ref[2:3]).astype(BF16)

    def feature_pull(value, grad):
        a, b = factors(value)
        scaled = grad * rows_ref[2:3]
        return nt((scaled * b).astype(BF16), ra_ref[...]) + nt((scaled * a).astype(BF16), rb_ref[...])

    def loop(n, body):
        def step(i, carry):
            body(i)
            return carry

        lax.fori_loop(0, n, step, 0)

    hcols = [slice(h * DV, (h + 1) * DV) for h in range(HL)]

    own_v.wait()
    arrived(vext.at[pl.ds(0, 16)], "halo")

    def front(ci):
        rows = span(ci)
        before = vext[pl.ds(pl.multiple_of(ci * CH, CH), 16)].astype(F32)
        before = jnp.where((ctx > 0) | (ci > 0), before, 0.0)
        here = vext[pl.ds(pl.multiple_of(ci * CH + 16, 16), CH)].astype(F32)
        back1 = jnp.where(row_id == 0, before[15:16], pltpu.roll(here, 1, 0))
        back2 = jnp.where(
            row_id == 0, before[14:15], jnp.where(row_id == 1, before[15:16], pltpu.roll(here, 2, 0))
        )
        mixed = cw_ref[0:1] * here + cw_ref[1:2] * back1 + cw_ref[2:3] * back2
        mixed = mixed.astype(BF16)
        u[rows] = mixed
        qf[rows] = features(q_ref[rows])
        kk = features(k_ref[rows])
        kf[rows] = kk
        for cols in hcols:
            sc[ci, :, cols] = tn(kk[:, cols], mixed[:, cols])
        zc[pl.ds(ci, 1)] = jnp.sum(kk.astype(F32), axis=0, keepdims=True)

    loop(NC, front)

    def scan_open(tag, states, norms, s_send, s_line):
        for j in range(4):
            cols = slice(j * 128, (j + 1) * 128)
            total = states[0, 0:FR, cols]
            for ci in range(1, NC):
                total = total + states[ci, 0:FR, cols]
            norm = jnp.sum(norms[0:NC, cols], axis=0, keepdims=True)
            s_send[j, 0:FR] = total.astype(BF16)
            s_send[j, FR:SR] = jnp.broadcast_to(norm, (16, 128)).astype(BF16)
        for d in range(1, 4):
            send(s_send.at[(z + d) % 4], s_line.at[z], (tag, 1, d), zs[d])
        s_line[z] = s_send[z]

    def scan_middle(tag, s_line, s_tot, s_tots):
        for d in range(1, 4):
            arrived(s_line.at[(z + 4 - d) % 4], (tag, 1, d))
        total = s_line[0].astype(F32)
        for i in range(1, 4):
            total = total + s_line[i].astype(F32)
        s_tot[...] = total.astype(BF16)
        for d in range(1, 4):
            send(s_tot, s_tots.at[x], (tag, 2, d), xs[d])

    def scan_close(tag, s_line, s_tots, s_back, s_prior, backward):
        for d in range(1, 4):
            arrived(s_tots.at[(x + 4 - d) % 4], (tag, 2, d))
        run = jnp.zeros((SR, 128), F32)
        for i in range(4):
            wanted = (i > x) if backward else (i < x)
            run = run + jnp.where(wanted, s_tots[i].astype(F32), 0.0)
        for i in reversed(range(4)) if backward else range(4):
            s_back[i] = run.astype(BF16)
            run = run + s_line[i].astype(F32)
        for d in range(1, 4):
            send(s_back.at[(z + d) % 4], s_prior.at[z], (tag, 3, d), zs[d])
        s_prior[z] = s_back[z]

    def scan_end(tag, states, norms, s_prior, to_states, to_norms, backward):
        for d in range(1, 4):
            arrived(s_prior.at[(z + 4 - d) % 4], (tag, 3, d))
        for j in range(4):
            cols = slice(j * 128, (j + 1) * 128)
            run = s_prior[j, 0:FR].astype(F32)
            norm = s_prior[j, FR:SR].astype(F32)[0:1]
            for ci in reversed(range(NC)) if backward else range(NC):
                to_states[ci, 0:FR, cols] = run.astype(BF16)
                to_states[ci, FR:FW, cols] = jnp.zeros((FW - FR, 128), BF16)
                to_norms[ci : ci + 1, cols] = norm
                run = run + states[ci, 0:FR, cols]
                norm = norm + norms[ci : ci + 1, cols]

    scan_open("f", sc, zc, f_send, f_line)

    def scores_of(ci, h):
        s = nt(head_of(q_ref[span(ci)], h), k_ref[span(ci)]) * (1.0 / math.sqrt(FEAT))
        return s, jnp.where(causal, 1.0 + s + 0.5 * s * s, 0.0)

    def inside(ci):
        rows = span(ci)
        for h, cols in enumerate(hcols):
            _, weight = scores_of(ci, h)
            num[rows, cols] = nn(weight.astype(BF16), u[rows, cols])
            den[h, rows] = jnp.sum(weight, axis=1, keepdims=True)

    loop(NC, inside)
    scan_middle("f", f_line, f_tot, f_tots)

    def pull(block, start=False):
        wrows = pl.ds(pl.multiple_of(block * COLS, COLS), COLS)

        def part(r):
            rows = span(r, HALF)
            got = nn(cfull[block, rows], w[wrows])
            ga[rows] = got if start else ga[rows] + got

        loop(2, part)

    own_c.wait()
    own_w.wait()
    pull(mine, True)

    arrived(cfull.at[from_l, first], "r0")
    send(cfull.at[from_l, first], cfull.at[from_l, first], "fr", to_right)
    send(cfull.at[from_l, first], cfull.at[from_l, first], "pl0", partner)
    arrived(cfull.at[from_r, second], "l1")
    send(cfull.at[from_r, second], cfull.at[from_r, second], "fl", to_left)
    send(cfull.at[from_r, second], cfull.at[from_r, second], "pr1", partner)

    scan_close("f", f_line, f_tots, f_back, f_prior, False)
    other = y * 2 + 1 - c
    arrived(cfull.at[other], "p")
    pull(other)

    scan_end("f", sc, zc, f_prior, sb, zb, False)

    def finish(ci):
        rows = span(ci)
        pieces = []
        for h, cols in enumerate(hcols):
            qh = qf[rows, cols]
            n = num[rows, cols] + nn(qh, sb[ci, :, cols])
            below = den[h, rows] + jnp.sum(qh.astype(F32) * zb[pl.ds(ci, 1), cols], axis=1, keepdims=True)
            r = 1.0 / below
            num[rows, cols] = n
            den[h, rows] = r
            pieces.append((n * r).astype(BF16))
            att[rows, cols] = pieces[-1]
        for h in range(HL):
            att_t[h * DV : (h + 1) * DV, rows] = pieces[h].T

    loop(NC, finish)
    send(att, attp, "att", partner)

    arrived(cfull.at[from_l, second], "r1")
    send(cfull.at[from_l, second], cfull.at[from_l, second], "pl1", partner)
    arrived(cfull.at[from_r, first], "l0")
    send(cfull.at[from_r, first], cfull.at[from_r, first], "pr0", partner)
    pull(from_l)

    for yy in range(4):
        arrived(wx.at[yy], ("w", yy))
    arrived(attp, "att")

    def project(yy, r):
        rows = pl.ds(r * HALF, HALF)
        wrows = pl.ds(pl.multiple_of((yy * 2 + c) * COLS, COLS), COLS)
        return nt(att[rows], w[wrows]) + nt(attp[rows], wx[yy])

    so[0, first] = project(yo, 0).astype(BF16)
    send(so.at[0, first], rhalf.at[0], "oh0", to_right)
    so[0, second] = project(yo, 1).astype(BF16)
    send(so.at[0, second], rhalf.at[1], "oh1", to_left)
    pull(from_r)

    arrived(cfull.at[from_o, first], "fr")
    send(cfull.at[from_o, first], cfull.at[from_o, first], "po0", partner)
    arrived(cfull.at[from_o, second], "fl")
    send(cfull.at[from_o, second], cfull.at[from_o, second], "po1", partner)
    pull(from_o)

    p_l, p_r, p_o = yl * 2 + 1 - c, yr * 2 + 1 - c, yo * 2 + 1 - c
    arrived(cfull.at[p_l, first], "pl0")
    arrived(cfull.at[p_l, second], "pl1")
    pull(p_l)
    arrived(cfull.at[p_r, first], "pr0")
    arrived(cfull.at[p_r, second], "pr1")
    pull(p_r)
    arrived(cfull.at[p_o, first], "po0")
    arrived(cfull.at[p_o, second], "po1")
    pull(p_o)

    def back_states(ci):
        rows = span(ci)
        for h, cols in enumerate(hcols):
            g = ga[rows, cols].astype(BF16)
            gab[rows, cols] = g
            r = den[h, rows]
            dd = -jnp.sum(g.astype(F32) * num[rows, cols], axis=1, keepdims=True) * r * r
            gd[h, rows] = dd
            qh = qf[rows, cols].astype(F32)
            sc[ci, :, cols] = tn((qh * r).astype(BF16), g)
            gzc[pl.ds(ci, 1), cols] = jnp.sum(qh * dd, axis=0, keepdims=True)

    loop(NC, back_states)
    scan_open("b", sc, gzc, b_send, b_line)

    so[1, second] = project(yr, 1).astype(BF16)
    send(so.at[1, second], rfull.at[0, second], "of1", to_right)
    so[2, first] = project(yl, 0).astype(BF16)
    send(so.at[2, first], rfull.at[1, first], "of2", to_left)
    scan_middle("b", b_line, b_tot, b_tots)
    arrived(rhalf.at[0], "oh0")
    so[1, first] = (project(yr, 0) + rhalf[0].astype(F32)).astype(BF16)
    send(so.at[1, first], rfull.at[0, first], "of0", to_right)
    arrived(rhalf.at[1], "oh1")
    so[2, second] = (project(yl, 1) + rhalf[1].astype(F32)).astype(BF16)
    send(so.at[2, second], rfull.at[1, second], "of3", to_left)

    along_x = c == 0
    pa = jnp.where(along_x, x, z)
    pb = jnp.where(along_x, z, x)

    def at(a, b):
        return {"ctx": jnp.where(along_x, a * 4 + b, b * 4 + a), "tp": tp}

    ar, al, ao = (pa + 1) % 4, (pa + 3) % 4, (pa + 2) % 4
    br, bl, bo = (pb + 1) % 4, (pb + 3) % 4, (pb + 2) % 4

    def tile(a, b):
        i = jnp.where(along_x, a * 4 + b, b * 4 + a)
        cols = pl.ds(pl.multiple_of((i % 2) * 256, 256), 256)
        return nn(att_t[...], cfull[i // 2, :, cols])

    def opposite(b):
        gs[0, b] = tile(ao, b).astype(BF16)

    loop(4, opposite)
    low, high = pl.ds(0, 2), pl.ds(2, 2)
    send(gs.at[0, low], ghalf.at[0], "gh0", at(ar, pb))
    send(gs.at[0, high], ghalf.at[1], "gh1", at(al, pb))
    scan_close("b", b_line, b_tots, b_back, b_prior, True)

    def near(b):
        gs[1, b + 2] = tile(ar, b + 2).astype(BF16)
        gs[2, b] = tile(al, b).astype(BF16)

    loop(2, near)
    send(gs.at[1, high], gfull.at[0, high], "gf1", at(ar, pb))
    send(gs.at[2, low], gfull.at[1, low], "gf2", at(al, pb))
    arrived(ghalf.at[0], "gh0")
    arrived(ghalf.at[1], "gh1")

    def joined(b):
        gs[1, b] = (tile(ar, b) + ghalf[0, b].astype(F32)).astype(BF16)
        gs[2, b + 2] = (tile(al, b + 2) + ghalf[1, b].astype(F32)).astype(BF16)

    loop(2, joined)
    send(gs.at[1, low], gfull.at[0, low], "gf0", at(ar, pb))
    send(gs.at[2, high], gfull.at[1, high], "gf3", at(al, pb))

    def back_inside(ci):
        rows = span(ci)
        gq = jnp.zeros((CH, HL * FEAT), F32)
        gk = jnp.zeros((CH, HL * FEAT), F32)
        grads = []
        for h, cols in enumerate(hcols):
            s, weight = scores_of(ci, h)
            r, dd, g = den[h, rows], gd[h, rows], gab[rows, cols]
            m = nt(g, u[rows, cols]) * r + dd
            m = jnp.where(causal, m * (1.0 + s) * (1.0 / math.sqrt(FEAT)), 0.0).astype(BF16)
            gq = gq + nn(m, head_of(k_ref[rows], h))
            gk = gk + tn(m, head_of(q_ref[rows], h))
            gm[rows, cols] = tn((weight * r).astype(BF16), g)
            grads.append(nt(g, sb[ci, :, cols]) * r + dd * zb[pl.ds(ci, 1), cols])
        gks[rows] = gk
        gq = gq + feature_pull(q_ref[rows], jnp.concatenate(grads, axis=1))
        gq_ref[rows] = gq.astype(BF16)

    loop(NC, back_inside)

    scan_end("b", sc, gzc, b_prior, gb, gzb, True)

    def back_after(ci):
        rows = span(ci)
        grads = []
        for h, cols in enumerate(hcols):
            state = gb[ci, :, cols]
            gm[rows, cols] = gm[rows, cols] + nn(kf[rows, cols], state)
            grads.append(nt(u[rows, cols], state) + gzb[pl.ds(ci, 1), cols])
        gk = gks[rows] + feature_pull(k_ref[rows], jnp.concatenate(grads, axis=1))
        gk_ref[rows] = gk.astype(BF16)

    loop(NC, back_after)
    send(gm.at[pl.ds(0, 8)], gm.at[pl.ds(TOK, 8)], "ghalo", earlier)

    arrived(gfull.at[0, high], "gf1")
    arrived(gfull.at[1, low], "gf2")
    arrived(gfull.at[0, low], "gf0")
    arrived(gfull.at[1, high], "gf3")

    def own_tile(b):
        ph[b] = tile(pa, b) + gfull[0, b].astype(F32) + gfull[1, b].astype(F32)

    loop(4, own_tile)
    top, bottom = pl.ds(0, 256), pl.ds(256, 256)
    hs[0] = ph[bo].astype(BF16)
    send(hs.at[0, top], hhalf.at[0], "hh0", at(pa, br))
    send(hs.at[0, bottom], hhalf.at[1], "hh1", at(pa, bl))
    hs[1, bottom] = ph[br, bottom].astype(BF16)
    send(hs.at[1, bottom], hfull.at[0, bottom], "hf1", at(pa, br))
    hs[2, top] = ph[bl, top].astype(BF16)
    send(hs.at[2, top], hfull.at[1, top], "hf2", at(pa, bl))

    arrived(gm.at[pl.ds(TOK, 8)], "ghalo")

    def tail(ci):
        rows = span(ci)
        here = gm[rows]
        after = gm[pl.ds(pl.multiple_of(ci * CH + CH, 8), 8)]
        after = jnp.where((ctx < 15) | (ci < NC - 1), after, 0.0)
        next1 = jnp.where(row_id == CH - 1, after[0:1], pltpu.roll(here, CH - 1, 0))
        next2 = jnp.where(
            row_id == CH - 1, after[1:2], jnp.where(row_id == CH - 2, after[0:1], pltpu.roll(here, CH - 2, 0))
        )
        total = cw_ref[0:1] * here + cw_ref[1:2] * next1 + cw_ref[2:3] * next2
        gv_ref[rows] = total.astype(BF16)

    loop(NC, tail)

    arrived(hhalf.at[0], "hh0")
    hs[1, top] = (ph[br, top] + hhalf[0].astype(F32)).astype(BF16)
    send(hs.at[1, top], hfull.at[0, top], "hf0", at(pa, br))
    arrived(hhalf.at[1], "hh1")
    hs[2, bottom] = (ph[bl, bottom] + hhalf[1].astype(F32)).astype(BF16)
    send(hs.at[2, bottom], hfull.at[1, bottom], "hf3", at(pa, bl))

    arrived(rfull.at[0, second], "of1")
    arrived(rfull.at[1, second], "of3")
    out_ref[second] = (project(y, 1) + rfull[0, second].astype(F32) + rfull[1, second].astype(F32)).astype(BF16)
    arrived(rfull.at[1, first], "of2")
    arrived(rfull.at[0, first], "of0")
    out_ref[first] = (project(y, 0) + rfull[0, first].astype(F32) + rfull[1, first].astype(F32)).astype(BF16)

    for name, side, rows in (("hf1", 0, bottom), ("hf2", 1, top), ("hf0", 0, top), ("hf3", 1, bottom)):
        arrived(hfull.at[side, rows], name)
    total = ph[pb] + hfull[0].astype(F32) + hfull[1].astype(F32)
    gw_ref[...] = total.T

    for copy in pending:
        copy.wait_send()


SEMS = 64


def body(queries, keys, values, conv_weight, w_out, cotangent):
    first, second, rows = feature_tables()
    vmem = pl.BlockSpec(memory_space=pltpu.VMEM)
    hbm = pl.BlockSpec(memory_space=pl.ANY)
    shapes = [
        ((8, TOK, COLS), BF16), ((D, COLS), BF16), ((4, COLS, COLS), BF16), ((TOK + 16, COLS), BF16),
        ((TOK, COLS), BF16), ((TOK, HL * FW), BF16), ((TOK, HL * FW), BF16),
        ((TOK, COLS), F32), ((HL, TOK, 1), F32), ((HL, TOK, 1), F32),
        ((TOK, COLS), BF16), ((TOK, COLS), BF16), ((COLS, TOK), BF16),
        ((TOK, COLS), F32), ((TOK, COLS), BF16), ((TOK + 8, COLS), F32), ((TOK, HL * FEAT), F32),
        ((NC, FW, COLS), F32), ((NC, FW, COLS), BF16), ((NC, FW, COLS), BF16),
        ((8, HL * FW), F32), ((8, HL * FW), F32), ((8, HL * FW), F32), ((8, HL * FW), F32),
    ]
    for _ in range(2):
        shapes += [
            ((4, SR, 128), BF16), ((4, SR, 128), BF16), ((SR, 128), BF16),
            ((4, SR, 128), BF16), ((4, SR, 128), BF16), ((4, SR, 128), BF16),
        ]
    shapes += [
        ((3, TOK, COLS), BF16), ((2, HALF, COLS), BF16), ((2, TOK, COLS), BF16),
        ((3, 4, COLS, 256), BF16), ((2, 2, COLS, 256), BF16), ((2, 4, COLS, 256), BF16),
        ((4, COLS, 256), F32), ((3, COLS, 256), BF16), ((2, 256, 256), BF16), ((2, COLS, 256), BF16),
    ]
    return pl.pallas_call(
        kernel,
        out_shape=(
            jax.ShapeDtypeStruct((TOK, COLS), BF16),
            jax.ShapeDtypeStruct((TOK, HL * FEAT), BF16),
            jax.ShapeDtypeStruct((TOK, HL * FEAT), BF16),
            jax.ShapeDtypeStruct((TOK, COLS), BF16),
            jax.ShapeDtypeStruct((256, COLS), F32),
        ),
        in_specs=[vmem] * 6 + [hbm] * 3,
        out_specs=(vmem,) * 5,
        scratch_shapes=[pltpu.VMEM(s, t) for s, t in shapes]
        + [pltpu.SemaphoreType.DMA((SEMS,)), pltpu.SemaphoreType.DMA((SEMS,)), pltpu.SemaphoreType.DMA((3,))],
        compiler_params=pltpu.CompilerParams(
            collective_id=0, has_side_effects=True, vmem_limit_bytes=67043328
        ),
        name="based_layer",
    )(
        queries, keys, conv_weight, jnp.asarray(first, BF16), jnp.asarray(second, BF16),
        jnp.asarray(rows, F32), values, w_out, cotangent,
    )


def solution(mesh):
    split = P("ctx", "tp")
    return jax.shard_map(
        body,
        mesh=mesh,
        in_specs=(split, split, split, P(None, "tp"), P(None, "tp"), split),
        out_specs=(split,) * 5,
        check_vma=False,
    )
```

```python
import functools
import math

import jax
import jax.numpy as jnp
import numpy as np
from jax import lax
from jax.experimental import pallas as pl
from jax.experimental.pallas import tpu as pltpu
from jax.sharding import PartitionSpec as P

MESH = pl.DeviceIdType.MESH
F32 = jnp.float32
BF16 = jnp.bfloat16

FEAT = 16
HL = 2
DV = 256
COLS = HL * DV
TOK = 1024
D = 4096
CH = 256
NC = TOK // CH
HALF = TOK // 2
FW = 256
FR = 160
SR = FR + 16


def nn(a, b):
    return lax.dot_general(a, b, (((1,), (0,)), ((), ())), preferred_element_type=F32)


def nt(a, b):
    return lax.dot_general(a, b, (((1,), (1,)), ((), ())), preferred_element_type=F32)


def tn(a, b):
    return lax.dot_general(a, b, (((0,), (0,)), ((), ())), preferred_element_type=F32)


def feature_tables():
    pairs = [(FEAT, FEAT, 1.0)]
    pairs += [(i, FEAT, 1.0 / math.sqrt(math.sqrt(FEAT))) for i in range(FEAT)]
    for i in range(FEAT):
        for j in range(i, FEAT):
            scale = 1.0 / (math.sqrt(2.0) * math.sqrt(FEAT))
            pairs.append((i, j, scale if i == j else scale * math.sqrt(2.0)))
    first = np.zeros((HL * FEAT, HL * FW), np.float32)
    second = np.zeros((HL * FEAT, HL * FW), np.float32)
    rows = np.zeros((8, HL * FW), np.float32)
    for h in range(HL):
        for col, (i, j, scale) in enumerate(pairs):
            at = h * FW + col
            if i == FEAT:
                rows[0, at] = 1.0
            else:
                first[h * FEAT + i, at] = 1.0
            if j == FEAT:
                rows[1, at] = 1.0
            else:
                second[h * FEAT + j, at] = 1.0
            rows[2, at] = scale
    return first, second, rows


def kernel(
    q_hbm, k_hbm, cw_hbm, ra_hbm, rb_hbm, rows_hbm, val_hbm, w_hbm, cot_hbm,
    out_hbm, gq_hbm, gk_hbm, gv_hbm, gw_hbm,
    q_t, k_t, cw_ref, ra_ref, rb_ref, rows_ref, q_ref, k_ref, gq_t, gk_t, gw_ref,
    cfull, w, wx, vext, u, qf, kf, num, den, gd, att, attp, att_t, ga, gab, gm, gks,
    sc, sb, gb, zc, zb, gzc, gzb,
    f_send, f_line, f_tot, f_tots, f_back, f_prior,
    b_send, b_line, b_tot, b_tots, b_back, b_prior,
    so, rhalf, rfull, gs, ghalf, gfull, ph, hs, hhalf, hfull,
    send_sems, recv_sems, local_sems,
):
    ctx = lax.axis_index("ctx")
    tp = lax.axis_index("tp")
    x, z = ctx // 4, ctx % 4
    y, c = tp // 2, tp % 2
    yr, yl, yo = (y + 1) % 4, (y + 3) % 4, (y + 2) % 4
    partner = {"ctx": ctx, "tp": y * 2 + (1 - c)}
    to_right = {"ctx": ctx, "tp": yr * 2 + c}
    to_left = {"ctx": ctx, "tp": yl * 2 + c}
    later = {"ctx": (ctx + 1) % 16, "tp": tp}
    earlier = {"ctx": (ctx + 15) % 16, "tp": tp}
    zs = [{"ctx": x * 4 + (z + d) % 4, "tp": tp} for d in range(4)]
    xs = [{"ctx": ((x + d) % 4) * 4 + z, "tp": tp} for d in range(4)]

    names = {}
    pending = []

    def number(name):
        return names.setdefault(name, len(names))

    def remote(src, dst, name, dev):
        i = number(name)
        return pltpu.make_async_remote_copy(
            src_ref=src, dst_ref=dst, send_sem=send_sems.at[i], recv_sem=recv_sems.at[i],
            device_id=dev, device_id_type=MESH,
        )

    def send(src, dst, name, dev):
        copy = remote(src, dst, name, dev)
        copy.start()
        pending.append(copy)

    def arrived(dst, name):
        remote(dst, dst, name, partner).wait_recv()

    own_w = pltpu.make_async_copy(w_hbm, w, local_sems.at[0])
    own_v = pltpu.make_async_copy(val_hbm, vext.at[pl.ds(16, TOK)], local_sems.at[1])
    own_c = pltpu.make_async_copy(cot_hbm, cfull.at[tp], local_sems.at[2])
    own_v.start()
    small = [
        pltpu.make_async_copy(a, b, local_sems.at[3 + i])
        for i, (a, b) in enumerate((
            (q_hbm, q_t), (k_hbm, k_t), (cw_hbm, cw_ref), (ra_hbm, ra_ref), (rb_hbm, rb_ref), (rows_hbm, rows_ref),
        ))
    ]
    for copy in small:
        copy.start()
    own_c.start()
    own_w.start()

    barrier = pltpu.get_barrier_semaphore()
    peers = [partner, to_right, to_left, later, earlier] + zs[1:] + xs[1:]
    for peer in peers:
        pl.semaphore_signal(barrier, inc=1, device_id=peer, device_id_type=MESH)
    pl.semaphore_wait(barrier, len(peers))

    first, second = pl.ds(0, HALF), pl.ds(HALF, HALF)
    mine, from_r, from_l, from_o = tp, yr * 2 + c, yl * 2 + c, yo * 2 + c
    send(val_hbm.at[pl.ds(TOK - 16, 16)], vext.at[pl.ds(0, 16)], "halo", later)
    send(cot_hbm.at[first], cfull.at[mine, first], "r0", to_right)
    send(cot_hbm.at[second], cfull.at[mine, second], "l1", to_left)
    send(cot_hbm.at[second], cfull.at[mine, second], "r1", to_right)
    send(cot_hbm.at[first], cfull.at[mine, first], "l0", to_left)
    send(cot_hbm, cfull.at[mine], "p", partner)
    for yy in range(4):
        rows = pl.ds(pl.multiple_of((yy * 2 + 1 - c) * COLS, COLS), COLS)
        send(w_hbm.at[rows], wx.at[yy], ("w", yy), partner)

    def span(i, size=CH):
        return pl.ds(pl.multiple_of(i * size, size), size)

    lane = lax.broadcasted_iota(jnp.int32, (CH, HL * FEAT), 1)
    row_id = lax.broadcasted_iota(jnp.int32, (CH, COLS), 0)
    causal = lax.broadcasted_iota(jnp.int32, (CH, CH), 0) >= lax.broadcasted_iota(jnp.int32, (CH, CH), 1)

    def head_of(value, h):
        return jnp.where(lane // FEAT == h, value, jnp.zeros_like(value))

    def factors(value):
        return nn(value, ra_ref[...]) + rows_ref[0:1], nn(value, rb_ref[...]) + rows_ref[1:2]

    def features(value):
        a, b = factors(value)
        return (a * b * rows_ref[2:3]).astype(BF16)

    def feature_pull(value, grad):
        a, b = factors(value)
        scaled = grad * rows_ref[2:3]
        return nt((scaled * b).astype(BF16), ra_ref[...]) + nt((scaled * a).astype(BF16), rb_ref[...])

    def loop(n, body):
        def step(i, carry):
            body(i)
            return carry

        lax.fori_loop(0, n, step, 0)

    hcols = [slice(h * DV, (h + 1) * DV) for h in range(HL)]

    for copy in small:
        copy.wait()
    own_v.wait()
    arrived(vext.at[pl.ds(0, 16)], "halo")

    def front(ci):
        rows = span(ci)
        before = vext[pl.ds(pl.multiple_of(ci * CH, CH), 16)].astype(F32)
        before = jnp.where((ctx > 0) | (ci > 0), before, 0.0)
        here = vext[pl.ds(pl.multiple_of(ci * CH + 16, 16), CH)].astype(F32)
        back1 = jnp.where(row_id == 0, before[15:16], pltpu.roll(here, 1, 0))
        back2 = jnp.where(
            row_id == 0, before[14:15], jnp.where(row_id == 1, before[15:16], pltpu.roll(here, 2, 0))
        )
        mixed = cw_ref[0:1] * here + cw_ref[1:2] * back1 + cw_ref[2:3] * back2
        mixed = mixed.astype(BF16)
        u[rows] = mixed
        qq, kk = q_t[:, rows].T, k_t[:, rows].T
        q_ref[rows], k_ref[rows] = qq, kk
        qf[rows] = features(qq)
        kk = features(kk)
        kf[rows] = kk
        for cols in hcols:
            sc[ci, :, cols] = tn(kk[:, cols], mixed[:, cols])
        zc[pl.ds(ci, 1)] = jnp.sum(kk.astype(F32), axis=0, keepdims=True)

    loop(NC, front)

    def scan_open(tag, states, norms, s_send, s_line):
        for j in range(4):
            cols = slice(j * 128, (j + 1) * 128)
            total = states[0, 0:FR, cols]
            for ci in range(1, NC):
                total = total + states[ci, 0:FR, cols]
            norm = jnp.sum(norms[0:NC, cols], axis=0, keepdims=True)
            s_send[j, 0:FR] = total.astype(BF16)
            s_send[j, FR:SR] = jnp.broadcast_to(norm, (16, 128)).astype(BF16)
        for d in range(1, 4):
            send(s_send.at[(z + d) % 4], s_line.at[z], (tag, 1, d), zs[d])
        s_line[z] = s_send[z]

    def scan_middle(tag, s_line, s_tot, s_tots):
        for d in range(1, 4):
            arrived(s_line.at[(z + 4 - d) % 4], (tag, 1, d))
        total = s_line[0].astype(F32)
        for i in range(1, 4):
            total = total + s_line[i].astype(F32)
        s_tot[...] = total.astype(BF16)
        for d in range(1, 4):
            send(s_tot, s_tots.at[x], (tag, 2, d), xs[d])

    def scan_close(tag, s_line, s_tots, s_back, s_prior, backward):
        for d in range(1, 4):
            arrived(s_tots.at[(x + 4 - d) % 4], (tag, 2, d))
        run = jnp.zeros((SR, 128), F32)
        for i in range(4):
            wanted = (i > x) if backward else (i < x)
            run = run + jnp.where(wanted, s_tots[i].astype(F32), 0.0)
        for i in reversed(range(4)) if backward else range(4):
            s_back[i] = run.astype(BF16)
            run = run + s_line[i].astype(F32)
        for d in range(1, 4):
            send(s_back.at[(z + d) % 4], s_prior.at[z], (tag, 3, d), zs[d])
        s_prior[z] = s_back[z]

    def scan_end(tag, states, norms, s_prior, to_states, to_norms, backward):
        for d in range(1, 4):
            arrived(s_prior.at[(z + 4 - d) % 4], (tag, 3, d))
        for j in range(4):
            cols = slice(j * 128, (j + 1) * 128)
            run = s_prior[j, 0:FR].astype(F32)
            norm = s_prior[j, FR:SR].astype(F32)[0:1]
            for ci in reversed(range(NC)) if backward else range(NC):
                to_states[ci, 0:FR, cols] = run.astype(BF16)
                to_states[ci, FR:FW, cols] = jnp.zeros((FW - FR, 128), BF16)
                to_norms[ci : ci + 1, cols] = norm
                run = run + states[ci, 0:FR, cols]
                norm = norm + norms[ci : ci + 1, cols]

    scan_open("f", sc, zc, f_send, f_line)

    def scores_of(ci, h):
        s = nt(head_of(q_ref[span(ci)], h), k_ref[span(ci)]) * (1.0 / math.sqrt(FEAT))
        return s, jnp.where(causal, 1.0 + s + 0.5 * s * s, 0.0)

    def inside(ci):
        rows = span(ci)
        for h, cols in enumerate(hcols):
            _, weight = scores_of(ci, h)
            num[rows, cols] = nn(weight.astype(BF16), u[rows, cols])
            den[h, rows] = jnp.sum(weight, axis=1, keepdims=True)

    loop(NC, inside)
    scan_middle("f", f_line, f_tot, f_tots)

    def pull(block, start=False):
        wrows = pl.ds(pl.multiple_of(block * COLS, COLS), COLS)

        def part(r):
            rows = span(r, HALF)
            got = nn(cfull[block, rows], w[wrows])
            ga[rows] = got if start else ga[rows] + got

        loop(2, part)

    own_c.wait()
    own_w.wait()
    pull(mine, True)

    arrived(cfull.at[from_l, first], "r0")
    send(cfull.at[from_l, first], cfull.at[from_l, first], "fr", to_right)
    send(cfull.at[from_l, first], cfull.at[from_l, first], "pl0", partner)
    arrived(cfull.at[from_r, second], "l1")
    send(cfull.at[from_r, second], cfull.at[from_r, second], "fl", to_left)
    send(cfull.at[from_r, second], cfull.at[from_r, second], "pr1", partner)

    scan_close("f", f_line, f_tots, f_back, f_prior, False)
    other = y * 2 + 1 - c
    arrived(cfull.at[other], "p")
    pull(other)

    scan_end("f", sc, zc, f_prior, sb, zb, False)

    def finish(ci):
        rows = span(ci)
        pieces = []
        for h, cols in enumerate(hcols):
            qh = qf[rows, cols]
            n = num[rows, cols] + nn(qh, sb[ci, :, cols])
            below = den[h, rows] + jnp.sum(qh.astype(F32) * zb[pl.ds(ci, 1), cols], axis=1, keepdims=True)
            r = 1.0 / below
            num[rows, cols] = n
            den[h, rows] = r
            pieces.append((n * r).astype(BF16))
            att[rows, cols] = pieces[-1]
        for h in range(HL):
            att_t[h * DV : (h + 1) * DV, rows] = pieces[h].T

    loop(NC, finish)
    send(att, attp, "att", partner)

    arrived(cfull.at[from_l, second], "r1")
    send(cfull.at[from_l, second], cfull.at[from_l, second], "pl1", partner)
    arrived(cfull.at[from_r, first], "l0")
    send(cfull.at[from_r, first], cfull.at[from_r, first], "pr0", partner)
    pull(from_l)

    for yy in range(4):
        arrived(wx.at[yy], ("w", yy))
    arrived(attp, "att")

    def project(yy, r):
        rows = pl.ds(r * HALF, HALF)
        wrows = pl.ds(pl.multiple_of((yy * 2 + c) * COLS, COLS), COLS)
        return nt(att[rows], w[wrows]) + nt(attp[rows], wx[yy])

    so[0, first] = project(yo, 0).astype(BF16)
    send(so.at[0, first], rhalf.at[0], "oh0", to_right)
    so[0, second] = project(yo, 1).astype(BF16)
    send(so.at[0, second], rhalf.at[1], "oh1", to_left)
    so[1, second] = project(yr, 1).astype(BF16)
    send(so.at[1, second], rfull.at[0, second], "of1", to_right)
    so[2, first] = project(yl, 0).astype(BF16)
    send(so.at[2, first], rfull.at[1, first], "of2", to_left)
    pull(from_r)

    p_l, p_r, p_o = yl * 2 + 1 - c, yr * 2 + 1 - c, yo * 2 + 1 - c
    arrived(cfull.at[p_l, first], "pl0")
    arrived(cfull.at[p_l, second], "pl1")
    pull(p_l)
    arrived(cfull.at[p_r, first], "pr0")
    arrived(cfull.at[p_r, second], "pr1")
    pull(p_r)
    arrived(cfull.at[from_o, first], "fr")
    send(cfull.at[from_o, first], cfull.at[from_o, first], "po0", partner)
    arrived(cfull.at[from_o, second], "fl")
    send(cfull.at[from_o, second], cfull.at[from_o, second], "po1", partner)
    pull(from_o)
    arrived(cfull.at[p_o, first], "po0")
    arrived(cfull.at[p_o, second], "po1")

    along_x = c == 0
    pa = jnp.where(along_x, x, z)
    pb = jnp.where(along_x, z, x)

    def at(a, b):
        return {"ctx": jnp.where(along_x, a * 4 + b, b * 4 + a), "tp": tp}

    ar, al, ao = (pa + 1) % 4, (pa + 3) % 4, (pa + 2) % 4
    br, bl, bo = (pb + 1) % 4, (pb + 3) % 4, (pb + 2) % 4

    def tile(a, b):
        i = jnp.where(along_x, a * 4 + b, b * 4 + a)
        cols = pl.ds(pl.multiple_of((i % 2) * 256, 256), 256)
        return nn(att_t[...], cfull[i // 2, :, cols])

    def opposite(b):
        gs[0, b] = tile(ao, b).astype(BF16)

    loop(4, opposite)
    low, high = pl.ds(0, 2), pl.ds(2, 2)
    send(gs.at[0, low], ghalf.at[0], "gh0", at(ar, pb))
    send(gs.at[0, high], ghalf.at[1], "gh1", at(al, pb))
    pull(p_o)

    def back_states(ci):
        rows = span(ci)
        for h, cols in enumerate(hcols):
            g = ga[rows, cols].astype(BF16)
            gab[rows, cols] = g
            r = den[h, rows]
            dd = -jnp.sum(g.astype(F32) * num[rows, cols], axis=1, keepdims=True) * r * r
            gd[h, rows] = dd
            qh = qf[rows, cols].astype(F32)
            sc[ci, :, cols] = tn((qh * r).astype(BF16), g)
            gzc[pl.ds(ci, 1), cols] = jnp.sum(qh * dd, axis=0, keepdims=True)

    loop(NC, back_states)
    scan_open("b", sc, gzc, b_send, b_line)

    def near(b):
        gs[1, b + 2] = tile(ar, b + 2).astype(BF16)
        gs[2, b] = tile(al, b).astype(BF16)

    loop(2, near)
    send(gs.at[1, high], gfull.at[0, high], "gf1", at(ar, pb))
    send(gs.at[2, low], gfull.at[1, low], "gf2", at(al, pb))
    scan_middle("b", b_line, b_tot, b_tots)

    arrived(rhalf.at[0], "oh0")
    so[1, first] = (project(yr, 0) + rhalf[0].astype(F32)).astype(BF16)
    send(so.at[1, first], rfull.at[0, first], "of0", to_right)
    arrived(rhalf.at[1], "oh1")
    so[2, second] = (project(yl, 1) + rhalf[1].astype(F32)).astype(BF16)
    send(so.at[2, second], rfull.at[1, second], "of3", to_left)
    scan_close("b", b_line, b_tots, b_back, b_prior, True)

    arrived(ghalf.at[0], "gh0")
    arrived(ghalf.at[1], "gh1")

    def joined(b):
        gs[1, b] = (tile(ar, b) + ghalf[0, b].astype(F32)).astype(BF16)
        gs[2, b + 2] = (tile(al, b + 2) + ghalf[1, b].astype(F32)).astype(BF16)

    loop(2, joined)
    send(gs.at[1, low], gfull.at[0, low], "gf0", at(ar, pb))
    send(gs.at[2, high], gfull.at[1, high], "gf3", at(al, pb))

    def back_inside(ci):
        rows = span(ci)
        gq = jnp.zeros((CH, HL * FEAT), F32)
        gk = jnp.zeros((CH, HL * FEAT), F32)
        grads = []
        for h, cols in enumerate(hcols):
            s, weight = scores_of(ci, h)
            r, dd, g = den[h, rows], gd[h, rows], gab[rows, cols]
            m = nt(g, u[rows, cols]) * r + dd
            m = jnp.where(causal, m * (1.0 + s) * (1.0 / math.sqrt(FEAT)), 0.0).astype(BF16)
            gq = gq + nn(m, head_of(k_ref[rows], h))
            gk = gk + tn(m, head_of(q_ref[rows], h))
            gm[rows, cols] = tn((weight * r).astype(BF16), g)
            grads.append(nt(g, sb[ci, :, cols]) * r + dd * zb[pl.ds(ci, 1), cols])
        gks[rows] = gk
        gq = gq + feature_pull(q_ref[rows], jnp.concatenate(grads, axis=1))
        gq_t[:, rows] = gq.T.astype(BF16)

    loop(NC, back_inside)

    scan_end("b", sc, gzc, b_prior, gb, gzb, True)

    def back_after(ci):
        rows = span(ci)
        grads = []
        for h, cols in enumerate(hcols):
            state = gb[ci, :, cols]
            gm[rows, cols] = gm[rows, cols] + nn(kf[rows, cols], state)
            grads.append(nt(u[rows, cols], state) + gzb[pl.ds(ci, 1), cols])
        gk = gks[rows] + feature_pull(k_ref[rows], jnp.concatenate(grads, axis=1))
        gk_t[:, rows] = gk.T.astype(BF16)

    loop(NC, back_after)
    send(gm.at[pl.ds(0, 8)], gm.at[pl.ds(TOK, 8)], "ghalo", earlier)
    results = []

    def give(src, dst):
        copy = pltpu.make_async_copy(src, dst, local_sems.at[9 + len(results)])
        copy.start()
        results.append(copy)

    give(gq_t, gq_hbm)
    give(gk_t, gk_hbm)

    def own_tile(b):
        ph[b] = tile(pa, b)

    loop(4, own_tile)

    def own_out(r):
        rows = span(r, HALF)
        wrows = pl.ds(pl.multiple_of((y * 2 + c) * COLS, COLS), COLS)
        ga[rows] = nt(att[rows], w[wrows]) + nt(attp[rows], wx[y])

    loop(2, own_out)

    arrived(gfull.at[0, high], "gf1")
    arrived(gfull.at[1, low], "gf2")
    arrived(gfull.at[0, low], "gf0")
    arrived(gfull.at[1, high], "gf3")

    def own_sum(b):
        ph[b] = ph[b] + gfull[0, b].astype(F32) + gfull[1, b].astype(F32)

    loop(4, own_sum)
    top, bottom = pl.ds(0, 256), pl.ds(256, 256)
    hs[0] = ph[bo].astype(BF16)
    send(hs.at[0, top], hhalf.at[0], "hh0", at(pa, br))
    send(hs.at[0, bottom], hhalf.at[1], "hh1", at(pa, bl))
    hs[1, bottom] = ph[br, bottom].astype(BF16)
    send(hs.at[1, bottom], hfull.at[0, bottom], "hf1", at(pa, br))
    hs[2, top] = ph[bl, top].astype(BF16)
    send(hs.at[2, top], hfull.at[1, top], "hf2", at(pa, bl))

    arrived(gm.at[pl.ds(TOK, 8)], "ghalo")

    def tail(ci):
        rows = span(ci)
        here = gm[rows]
        after = gm[pl.ds(pl.multiple_of(ci * CH + CH, 8), 8)]
        after = jnp.where((ctx < 15) | (ci < NC - 1), after, 0.0)
        next1 = jnp.where(row_id == CH - 1, after[0:1], pltpu.roll(here, CH - 1, 0))
        next2 = jnp.where(
            row_id == CH - 1, after[1:2], jnp.where(row_id == CH - 2, after[0:1], pltpu.roll(here, CH - 2, 0))
        )
        total = cw_ref[0:1] * here + cw_ref[1:2] * next1 + cw_ref[2:3] * next2
        gab[rows] = total.astype(BF16)

    loop(NC, tail)
    give(gab, gv_hbm)

    arrived(hhalf.at[0], "hh0")
    hs[1, top] = (ph[br, top] + hhalf[0].astype(F32)).astype(BF16)
    send(hs.at[1, top], hfull.at[0, top], "hf0", at(pa, br))
    arrived(hhalf.at[1], "hh1")
    hs[2, bottom] = (ph[bl, bottom] + hhalf[1].astype(F32)).astype(BF16)
    send(hs.at[2, bottom], hfull.at[1, bottom], "hf3", at(pa, bl))

    for sources, rows in (((("of1", 0), ("of3", 1)), second), ((("of2", 1), ("of0", 0)), first)):
        for name, side in sources:
            arrived(rfull.at[side, rows], name)
        attp[rows] = (ga[rows] + rfull[0, rows].astype(F32) + rfull[1, rows].astype(F32)).astype(BF16)
        give(attp.at[rows], out_hbm.at[rows])

    for name, side, rows in (("hf1", 0, bottom), ("hf2", 1, top), ("hf0", 0, top), ("hf3", 1, bottom)):
        arrived(hfull.at[side, rows], name)
    total = ph[pb] + hfull[0].astype(F32) + hfull[1].astype(F32)
    gw_ref[...] = total.T
    give(gw_ref, gw_hbm)
    for copy in results:
        copy.wait()

    for copy in pending:
        copy.wait_send()


SEMS = 64


def settle(*refs):
    n = len(refs) // 3
    sources, targets, held, sems = refs[:n], refs[n : 2 * n], refs[2 * n : 3 * n], refs[3 * n]
    into = [pltpu.make_async_copy(a, b, sems.at[0, i]) for i, (a, b) in enumerate(zip(sources, held))]
    out = [pltpu.make_async_copy(a, b, sems.at[1, i]) for i, (a, b) in enumerate(zip(held, targets))]
    for copy in into:
        copy.start()
    for first, then in zip(into, out):
        first.wait()
        then.start()
    for copy in out:
        copy.wait()


def settled(arrays):
    hbm = pl.BlockSpec(memory_space=pl.ANY)
    shapes = [jax.ShapeDtypeStruct(a.shape, a.dtype) for a in arrays]
    return pl.pallas_call(
        settle,
        out_shape=tuple(shapes),
        in_specs=[hbm] * len(arrays),
        out_specs=(hbm,) * len(arrays),
        scratch_shapes=[pltpu.VMEM(a.shape, a.dtype) for a in arrays]
        + [pltpu.SemaphoreType.DMA((2, len(arrays)))],
        name="settle",
    )(*arrays)


def body(queries, keys, values, conv_weight, w_out, cotangent):
    first, second, rows = feature_tables()
    hbm = pl.BlockSpec(memory_space=pl.ANY)
    wide = HL * FEAT
    shapes = [
        ((wide, TOK), BF16), ((wide, TOK), BF16), ((3, COLS), F32), ((wide, HL * FW), BF16), ((wide, HL * FW), BF16),
        ((8, HL * FW), F32), ((TOK, wide), BF16), ((TOK, wide), BF16), ((wide, TOK), BF16), ((wide, TOK), BF16),
        ((256, COLS), F32),
        ((8, TOK, COLS), BF16), ((D, COLS), BF16), ((4, COLS, COLS), BF16), ((TOK + 16, COLS), BF16),
        ((TOK, COLS), BF16), ((TOK, HL * FW), BF16), ((TOK, HL * FW), BF16),
        ((TOK, COLS), F32), ((HL, TOK, 1), F32), ((HL, TOK, 1), F32),
        ((TOK, COLS), BF16), ((TOK, COLS), BF16), ((COLS, TOK), BF16),
        ((TOK, COLS), F32), ((TOK, COLS), BF16), ((TOK + 8, COLS), F32), ((TOK, HL * FEAT), F32),
        ((NC, FW, COLS), F32), ((NC, FW, COLS), BF16), ((NC, FW, COLS), BF16),
        ((8, HL * FW), F32), ((8, HL * FW), F32), ((8, HL * FW), F32), ((8, HL * FW), F32),
    ]
    for _ in range(2):
        shapes += [
            ((4, SR, 128), BF16), ((4, SR, 128), BF16), ((SR, 128), BF16),
            ((4, SR, 128), BF16), ((4, SR, 128), BF16), ((4, SR, 128), BF16),
        ]
    shapes += [
        ((3, TOK, COLS), BF16), ((2, HALF, COLS), BF16), ((2, TOK, COLS), BF16),
        ((3, 4, COLS, 256), BF16), ((2, 2, COLS, 256), BF16), ((2, 4, COLS, 256), BF16),
        ((4, COLS, 256), F32), ((3, COLS, 256), BF16), ((2, 256, 256), BF16), ((2, COLS, 256), BF16),
    ]
    out, gq, gk, gv, gw = settled(pl.pallas_call(
        kernel,
        out_shape=(
            jax.ShapeDtypeStruct((TOK, COLS), BF16),
            jax.ShapeDtypeStruct((HL * FEAT, TOK), BF16),
            jax.ShapeDtypeStruct((HL * FEAT, TOK), BF16),
            jax.ShapeDtypeStruct((TOK, COLS), BF16),
            jax.ShapeDtypeStruct((256, COLS), F32),
        ),
        in_specs=[hbm] * 9,
        out_specs=(hbm,) * 5,
        scratch_shapes=[pltpu.VMEM(s, t) for s, t in shapes]
        + [pltpu.SemaphoreType.DMA((SEMS,)), pltpu.SemaphoreType.DMA((SEMS,)), pltpu.SemaphoreType.DMA((16,))],
        compiler_params=pltpu.CompilerParams(
            collective_id=0, has_side_effects=True, vmem_limit_bytes=67043328
        ),
        name="based_layer",
    )(
        queries.T, keys.T, conv_weight, jnp.asarray(first, BF16), jnp.asarray(second, BF16),
        jnp.asarray(rows, F32), values, w_out, cotangent,
    ))
    return out, gq.T, gk.T, gv, gw


def solution(mesh):
    split = P("ctx", "tp")
    return jax.shard_map(
        body,
        mesh=mesh,
        in_specs=(split, split, split, P(None, "tp"), P(None, "tp"), split),
        out_specs=(split,) * 5,
        check_vma=False,
    )
```

```python
import functools
import math

import jax
import jax.numpy as jnp
import numpy as np
from jax import lax
from jax.experimental import pallas as pl
from jax.experimental.pallas import tpu as pltpu
from jax.sharding import PartitionSpec as P

MESH = pl.DeviceIdType.MESH
F32 = jnp.float32
BF16 = jnp.bfloat16

FEAT = 16
HL = 2
DV = 256
COLS = HL * DV
TOK = 1024
D = 4096
CH = 256
NC = TOK // CH
HALF = TOK // 2
FW = 256
FR = 160
SR = FR + 16


def nn(a, b):
    return lax.dot_general(a, b, (((1,), (0,)), ((), ())), preferred_element_type=F32)


def nt(a, b):
    return lax.dot_general(a, b, (((1,), (1,)), ((), ())), preferred_element_type=F32)


def tn(a, b):
    return lax.dot_general(a, b, (((0,), (0,)), ((), ())), preferred_element_type=F32)


def feature_tables():
    pairs = [(FEAT, FEAT, 1.0)]
    pairs += [(i, FEAT, 1.0 / math.sqrt(math.sqrt(FEAT))) for i in range(FEAT)]
    for i in range(FEAT):
        for j in range(i, FEAT):
            scale = 1.0 / (math.sqrt(2.0) * math.sqrt(FEAT))
            pairs.append((i, j, scale if i == j else scale * math.sqrt(2.0)))
    first = np.zeros((HL * FEAT, HL * FW), np.float32)
    second = np.zeros((HL * FEAT, HL * FW), np.float32)
    rows = np.zeros((8, HL * FW), np.float32)
    for h in range(HL):
        for col, (i, j, scale) in enumerate(pairs):
            at = h * FW + col
            if i == FEAT:
                rows[0, at] = 1.0
            else:
                first[h * FEAT + i, at] = 1.0
            if j == FEAT:
                rows[1, at] = 1.0
            else:
                second[h * FEAT + j, at] = 1.0
            rows[2, at] = scale
    return first, second, rows


def kernel(
    q_hbm, k_hbm, cw_hbm, ra_hbm, rb_hbm, rows_hbm, val_hbm, w_hbm, cot_hbm,
    out_hbm, gq_hbm, gk_hbm, gv_hbm, gw_hbm,
    q_t, k_t, cw_ref, ra_ref, rb_ref, rows_ref, q_ref, k_ref, gq_t, gk_t, gw_ref,
    cfull, w, wx, vext, u, qf, kf, num, den, gd, att, attp, att_t, ga, gab, gm, gks,
    sc, sb, gb, zc, zb, gzc, gzb,
    f_send, f_line, f_tot, f_tots, f_back, f_prior,
    b_send, b_line, b_tot, b_tots, b_back, b_prior,
    so, oo, rhalf, rfull, gwt, ghalf, gfull, ph, hs, hhalf, hfull,
    send_sems, recv_sems, local_sems,
):
    ctx = lax.axis_index("ctx")
    tp = lax.axis_index("tp")
    x, z = ctx // 4, ctx % 4
    y, c = tp // 2, tp % 2
    yr, yl, yo = (y + 1) % 4, (y + 3) % 4, (y + 2) % 4
    partner = {"ctx": ctx, "tp": y * 2 + (1 - c)}
    to_right = {"ctx": ctx, "tp": yr * 2 + c}
    to_left = {"ctx": ctx, "tp": yl * 2 + c}
    later = {"ctx": (ctx + 1) % 16, "tp": tp}
    earlier = {"ctx": (ctx + 15) % 16, "tp": tp}
    zs = [{"ctx": x * 4 + (z + d) % 4, "tp": tp} for d in range(4)]
    xs = [{"ctx": ((x + d) % 4) * 4 + z, "tp": tp} for d in range(4)]

    names = {}
    pending = []

    def number(name):
        return names.setdefault(name, len(names))

    def remote(src, dst, name, dev):
        i = number(name)
        return pltpu.make_async_remote_copy(
            src_ref=src, dst_ref=dst, send_sem=send_sems.at[i], recv_sem=recv_sems.at[i],
            device_id=dev, device_id_type=MESH,
        )

    def send(src, dst, name, dev):
        copy = remote(src, dst, name, dev)
        copy.start()
        pending.append(copy)

    def arrived(dst, name):
        remote(dst, dst, name, partner).wait_recv()

    own_w = pltpu.make_async_copy(w_hbm, w, local_sems.at[0])
    own_v = pltpu.make_async_copy(val_hbm, vext.at[pl.ds(16, TOK)], local_sems.at[1])
    own_c = pltpu.make_async_copy(cot_hbm, cfull.at[tp], local_sems.at[2])
    own_v.start()
    small = [
        pltpu.make_async_copy(a, b, local_sems.at[3 + i])
        for i, (a, b) in enumerate((
            (q_hbm, q_t), (k_hbm, k_t), (cw_hbm, cw_ref), (ra_hbm, ra_ref), (rb_hbm, rb_ref), (rows_hbm, rows_ref),
        ))
    ]
    for copy in small:
        copy.start()
    own_c.start()
    own_w.start()

    barrier = pltpu.get_barrier_semaphore()
    peers = [partner, to_right, to_left, later, earlier] + zs[1:] + xs[1:]
    for peer in peers:
        pl.semaphore_signal(barrier, inc=1, device_id=peer, device_id_type=MESH)
    pl.semaphore_wait(barrier, len(peers))

    first, second = pl.ds(0, HALF), pl.ds(HALF, HALF)
    mine, from_r, from_l, from_o = tp, yr * 2 + c, yl * 2 + c, yo * 2 + c
    send(val_hbm.at[pl.ds(TOK - 16, 16)], vext.at[pl.ds(0, 16)], "halo", later)
    send(cot_hbm.at[first], cfull.at[mine, first], "r0", to_right)
    send(cot_hbm.at[second], cfull.at[mine, second], "l1", to_left)
    send(cot_hbm.at[second], cfull.at[mine, second], "r1", to_right)
    send(cot_hbm.at[first], cfull.at[mine, first], "l0", to_left)
    send(cot_hbm, cfull.at[mine], "p", partner)
    for yy in range(4):
        rows = pl.ds(pl.multiple_of((yy * 2 + 1 - c) * COLS, COLS), COLS)
        send(w_hbm.at[rows], wx.at[yy], ("w", yy), partner)

    def span(i, size=CH):
        return pl.ds(pl.multiple_of(i * size, size), size)

    lane = lax.broadcasted_iota(jnp.int32, (CH, HL * FEAT), 1)
    row_id = lax.broadcasted_iota(jnp.int32, (CH, COLS), 0)
    causal = lax.broadcasted_iota(jnp.int32, (CH, CH), 0) >= lax.broadcasted_iota(jnp.int32, (CH, CH), 1)

    def head_of(value, h):
        return jnp.where(lane // FEAT == h, value, jnp.zeros_like(value))

    def factors(value):
        return nn(value, ra_ref[...]) + rows_ref[0:1], nn(value, rb_ref[...]) + rows_ref[1:2]

    def features(value):
        a, b = factors(value)
        return (a * b * rows_ref[2:3]).astype(BF16)

    def feature_pull(value, grad):
        a, b = factors(value)
        scaled = grad * rows_ref[2:3]
        return nt((scaled * b).astype(BF16), ra_ref[...]) + nt((scaled * a).astype(BF16), rb_ref[...])

    def loop(n, body):
        def step(i, carry):
            body(i)
            return carry

        lax.fori_loop(0, n, step, 0)

    hcols = [slice(h * DV, (h + 1) * DV) for h in range(HL)]

    for copy in small:
        copy.wait()
    own_v.wait()
    arrived(vext.at[pl.ds(0, 16)], "halo")

    def front(ci):
        rows = span(ci)
        before = vext[pl.ds(pl.multiple_of(ci * CH, CH), 16)].astype(F32)
        before = jnp.where((ctx > 0) | (ci > 0), before, 0.0)
        here = vext[pl.ds(pl.multiple_of(ci * CH + 16, 16), CH)].astype(F32)
        back1 = jnp.where(row_id == 0, before[15:16], pltpu.roll(here, 1, 0))
        back2 = jnp.where(
            row_id == 0, before[14:15], jnp.where(row_id == 1, before[15:16], pltpu.roll(here, 2, 0))
        )
        mixed = cw_ref[0:1] * here + cw_ref[1:2] * back1 + cw_ref[2:3] * back2
        mixed = mixed.astype(BF16)
        u[rows] = mixed
        qq, kk = q_t[:, rows].T, k_t[:, rows].T
        q_ref[rows], k_ref[rows] = qq, kk
        qf[rows] = features(qq)
        kk = features(kk)
        kf[rows] = kk
        for cols in hcols:
            sc[ci, :, cols] = tn(kk[:, cols], mixed[:, cols])
        zc[pl.ds(ci, 1)] = jnp.sum(kk.astype(F32), axis=0, keepdims=True)

    loop(NC, front)

    def scan_open(tag, states, norms, s_send, s_line):
        for j in range(4):
            cols = slice(j * 128, (j + 1) * 128)
            total = states[0, 0:FR, cols]
            for ci in range(1, NC):
                total = total + states[ci, 0:FR, cols]
            norm = jnp.sum(norms[0:NC, cols], axis=0, keepdims=True)
            s_send[j, 0:FR] = total.astype(BF16)
            s_send[j, FR:SR] = jnp.broadcast_to(norm, (16, 128)).astype(BF16)
        for d in range(1, 4):
            send(s_send.at[(z + d) % 4], s_line.at[z], (tag, 1, d), zs[d])
        s_line[z] = s_send[z]

    def scan_middle(tag, s_line, s_tot, s_tots):
        for d in range(1, 4):
            arrived(s_line.at[(z + 4 - d) % 4], (tag, 1, d))
        total = s_line[0].astype(F32)
        for i in range(1, 4):
            total = total + s_line[i].astype(F32)
        s_tot[...] = total.astype(BF16)
        for d in range(1, 4):
            send(s_tot, s_tots.at[x], (tag, 2, d), xs[d])

    def scan_close(tag, s_line, s_tots, s_back, s_prior, backward):
        for d in range(1, 4):
            arrived(s_tots.at[(x + 4 - d) % 4], (tag, 2, d))
        run = jnp.zeros((SR, 128), F32)
        for i in range(4):
            wanted = (i > x) if backward else (i < x)
            run = run + jnp.where(wanted, s_tots[i].astype(F32), 0.0)
        for i in reversed(range(4)) if backward else range(4):
            s_back[i] = run.astype(BF16)
            run = run + s_line[i].astype(F32)
        for d in range(1, 4):
            send(s_back.at[(z + d) % 4], s_prior.at[z], (tag, 3, d), zs[d])
        s_prior[z] = s_back[z]

    def scan_end(tag, states, norms, s_prior, to_states, to_norms, backward):
        for d in range(1, 4):
            arrived(s_prior.at[(z + 4 - d) % 4], (tag, 3, d))
        for j in range(4):
            cols = slice(j * 128, (j + 1) * 128)
            run = s_prior[j, 0:FR].astype(F32)
            norm = s_prior[j, FR:SR].astype(F32)[0:1]
            for ci in reversed(range(NC)) if backward else range(NC):
                to_states[ci, 0:FR, cols] = run.astype(BF16)
                to_states[ci, FR:FW, cols] = jnp.zeros((FW - FR, 128), BF16)
                to_norms[ci : ci + 1, cols] = norm
                run = run + states[ci, 0:FR, cols]
                norm = norm + norms[ci : ci + 1, cols]

    scan_open("f", sc, zc, f_send, f_line)

    def scores_of(ci, h):
        s = nt(head_of(q_ref[span(ci)], h), k_ref[span(ci)]) * (1.0 / math.sqrt(FEAT))
        return s, jnp.where(causal, 1.0 + s + 0.5 * s * s, 0.0)

    def inside(ci):
        rows = span(ci)
        for h, cols in enumerate(hcols):
            _, weight = scores_of(ci, h)
            num[rows, cols] = nn(weight.astype(BF16), u[rows, cols])
            den[h, rows] = jnp.sum(weight, axis=1, keepdims=True)

    loop(NC, inside)
    scan_middle("f", f_line, f_tot, f_tots)

    def pull(block, start=False):
        wrows = pl.ds(pl.multiple_of(block * COLS, COLS), COLS)

        def part(r):
            rows = span(r, HALF)
            got = nn(cfull[block, rows], w[wrows])
            ga[rows] = got if start else ga[rows] + got

        loop(2, part)

    own_c.wait()
    own_w.wait()
    pull(mine, True)

    arrived(cfull.at[from_l, first], "r0")
    send(cfull.at[from_l, first], cfull.at[from_l, first], "fr", to_right)
    send(cfull.at[from_l, first], cfull.at[from_l, first], "pl0", partner)
    arrived(cfull.at[from_r, second], "l1")
    send(cfull.at[from_r, second], cfull.at[from_r, second], "fl", to_left)
    send(cfull.at[from_r, second], cfull.at[from_r, second], "pr1", partner)

    scan_close("f", f_line, f_tots, f_back, f_prior, False)
    other = y * 2 + 1 - c
    arrived(cfull.at[other], "p")
    pull(other)

    scan_end("f", sc, zc, f_prior, sb, zb, False)

    def finish(ci):
        rows = span(ci)
        pieces = []
        for h, cols in enumerate(hcols):
            qh = qf[rows, cols]
            n = num[rows, cols] + nn(qh, sb[ci, :, cols])
            below = den[h, rows] + jnp.sum(qh.astype(F32) * zb[pl.ds(ci, 1), cols], axis=1, keepdims=True)
            r = 1.0 / below
            num[rows, cols] = n
            den[h, rows] = r
            pieces.append((n * r).astype(BF16))
            att[rows, cols] = pieces[-1]
        for h in range(HL):
            att_t[h * DV : (h + 1) * DV, rows] = pieces[h].T

    loop(NC, finish)
    send(att, attp, "att", partner)

    arrived(cfull.at[from_l, second], "r1")
    send(cfull.at[from_l, second], cfull.at[from_l, second], "pl1", partner)
    arrived(cfull.at[from_r, first], "l0")
    send(cfull.at[from_r, first], cfull.at[from_r, first], "pr0", partner)
    pull(from_l)

    for yy in range(4):
        arrived(wx.at[yy], ("w", yy))
    arrived(attp, "att")

    def project(yy, r):
        rows = pl.ds(r * HALF, HALF)
        wrows = pl.ds(pl.multiple_of((yy * 2 + c) * COLS, COLS), COLS)
        return nt(att[rows], w[wrows]) + nt(attp[rows], wx[yy])

    so[0, first] = project(yo, 0).astype(BF16)
    send(so.at[0, first], rhalf.at[0], "oh0", to_right)
    so[0, second] = project(yo, 1).astype(BF16)
    send(so.at[0, second], rhalf.at[1], "oh1", to_left)
    so[1, second] = project(yr, 1).astype(BF16)
    send(so.at[1, second], rfull.at[0, second], "of1", to_right)
    so[2, first] = project(yl, 0).astype(BF16)
    send(so.at[2, first], rfull.at[1, first], "of2", to_left)

    along_x = c == 0
    pa = jnp.where(along_x, x, z)
    pb = jnp.where(along_x, z, x)

    def at(a, b):
        return {"ctx": jnp.where(along_x, a * 4 + b, b * 4 + a), "tp": tp}

    ar, al, ao = (pa + 1) % 4, (pa + 3) % 4, (pa + 2) % 4
    br, bl, bo = (pb + 1) % 4, (pb + 3) % 4, (pb + 2) % 4

    def tiles(block):
        for half in range(2):
            i = 2 * block + half
            a, b = jnp.where(along_x, i // 4, i % 4), jnp.where(along_x, i % 4, i // 4)
            gwt[a, b] = nn(att_t[...], cfull[block, :, half * 256 : half * 256 + 256]).astype(BF16)

    p_l, p_r, p_o = yl * 2 + 1 - c, yr * 2 + 1 - c, yo * 2 + 1 - c
    pull(from_r)

    def ready(n):
        tiles(jnp.where(n == 0, mine, jnp.where(n == 1, other, jnp.where(n == 2, from_l, from_r))))

    loop(4, ready)
    arrived(cfull.at[p_l, first], "pl0")
    arrived(cfull.at[p_l, second], "pl1")
    pull(p_l)
    arrived(cfull.at[p_r, first], "pr0")
    arrived(cfull.at[p_r, second], "pr1")
    pull(p_r)

    def ready_too(n):
        tiles(jnp.where(n == 0, p_l, p_r))

    loop(2, ready_too)
    low, high = pl.ds(0, 2), pl.ds(2, 2)

    def known(group, upper):
        return jnp.where(along_x, group != yo, (yo < 2) if upper else (yo >= 2))

    gw_first = [
        (known(ao, False), gwt.at[ao, low], ghalf.at[0], "gh0", at(ar, pb)),
        (known(ao, True), gwt.at[ao, high], ghalf.at[1], "gh1", at(al, pb)),
        (known(ar, True), gwt.at[ar, high], gfull.at[0, high], "gf1", at(ar, pb)),
        (known(al, False), gwt.at[al, low], gfull.at[1, low], "gf2", at(al, pb)),
    ]

    def send_if(when, src, dst, name, dev):
        @pl.when(when)
        def _():
            remote(src, dst, name, dev).start()

    for when, *rest in gw_first[:4]:
        send_if(when, *rest)
    arrived(cfull.at[from_o, first], "fr")
    send(cfull.at[from_o, first], cfull.at[from_o, first], "po0", partner)
    arrived(cfull.at[from_o, second], "fl")
    send(cfull.at[from_o, second], cfull.at[from_o, second], "po1", partner)
    tiles(from_o)
    pull(from_o)
    arrived(cfull.at[p_o, first], "po0")
    arrived(cfull.at[p_o, second], "po1")
    tiles(p_o)
    for when, *rest in gw_first[:4]:
        send_if(jnp.logical_not(when), *rest)
        pending.append(remote(*rest))
    pull(p_o)

    def back_states(ci):
        rows = span(ci)
        for h, cols in enumerate(hcols):
            g = ga[rows, cols].astype(BF16)
            gab[rows, cols] = g
            r = den[h, rows]
            dd = -jnp.sum(g.astype(F32) * num[rows, cols], axis=1, keepdims=True) * r * r
            gd[h, rows] = dd
            qh = qf[rows, cols].astype(F32)
            sc[ci, :, cols] = tn((qh * r).astype(BF16), g)
            gzc[pl.ds(ci, 1), cols] = jnp.sum(qh * dd, axis=0, keepdims=True)

    loop(NC, back_states)
    scan_open("b", sc, gzc, b_send, b_line)
    so[1, first] = project(yr, 0).astype(BF16)
    so[2, second] = project(yl, 1).astype(BF16)

    def back_inside(ci):
        rows = span(ci)
        gq = jnp.zeros((CH, HL * FEAT), F32)
        gk = jnp.zeros((CH, HL * FEAT), F32)
        grads = []
        for h, cols in enumerate(hcols):
            s, weight = scores_of(ci, h)
            r, dd, g = den[h, rows], gd[h, rows], gab[rows, cols]
            m = nt(g, u[rows, cols]) * r + dd
            m = jnp.where(causal, m * (1.0 + s) * (1.0 / math.sqrt(FEAT)), 0.0).astype(BF16)
            gq = gq + nn(m, head_of(k_ref[rows], h))
            gk = gk + tn(m, head_of(q_ref[rows], h))
            gm[rows, cols] = tn((weight * r).astype(BF16), g)
            grads.append(nt(g, sb[ci, :, cols]) * r + dd * zb[pl.ds(ci, 1), cols])
        gks[rows] = gk
        gq = gq + feature_pull(q_ref[rows], jnp.concatenate(grads, axis=1))
        gq_t[:, rows] = gq.T.astype(BF16)

    loop(1, back_inside)
    scan_middle("b", b_line, b_tot, b_tots)

    arrived(rhalf.at[0], "oh0")
    so[1, first] = (so[1, first].astype(F32) + rhalf[0].astype(F32)).astype(BF16)
    send(so.at[1, first], rfull.at[0, first], "of0", to_right)
    arrived(rhalf.at[1], "oh1")
    so[2, second] = (so[2, second].astype(F32) + rhalf[1].astype(F32)).astype(BF16)
    send(so.at[2, second], rfull.at[1, second], "of3", to_left)

    def back_inside_rest(n):
        back_inside(n + 1)

    loop(1, back_inside_rest)
    scan_close("b", b_line, b_tots, b_back, b_prior, True)

    arrived(ghalf.at[0], "gh0")
    arrived(ghalf.at[1], "gh1")

    def joined(b):
        gwt[ar, b] = (gwt[ar, b].astype(F32) + ghalf[0, b].astype(F32)).astype(BF16)
        gwt[al, b + 2] = (gwt[al, b + 2].astype(F32) + ghalf[1, b].astype(F32)).astype(BF16)

    loop(2, joined)
    send(gwt.at[ar, low], gfull.at[0, low], "gf0", at(ar, pb))
    send(gwt.at[al, high], gfull.at[1, high], "gf3", at(al, pb))
    def back_inside_last(n):
        back_inside(n + 2)

    loop(2, back_inside_last)

    def own_out(r):
        rows = span(r, HALF)
        wrows = pl.ds(pl.multiple_of((y * 2 + c) * COLS, COLS), COLS)
        oo[rows] = nt(att[rows], w[wrows]) + nt(attp[rows], wx[y])

    loop(2, own_out)


    arrived(gfull.at[0, high], "gf1")
    arrived(gfull.at[1, low], "gf2")
    arrived(gfull.at[0, low], "gf0")
    arrived(gfull.at[1, high], "gf3")

    def own_sum(b):
        ph[b] = gwt[pa, b].astype(F32) + gfull[0, b].astype(F32) + gfull[1, b].astype(F32)

    loop(4, own_sum)
    top, bottom = pl.ds(0, 256), pl.ds(256, 256)
    hs[0] = ph[bo].astype(BF16)
    send(hs.at[0, top], hhalf.at[0], "hh0", at(pa, br))
    send(hs.at[0, bottom], hhalf.at[1], "hh1", at(pa, bl))
    hs[1, bottom] = ph[br, bottom].astype(BF16)
    send(hs.at[1, bottom], hfull.at[0, bottom], "hf1", at(pa, br))
    hs[2, top] = ph[bl, top].astype(BF16)
    send(hs.at[2, top], hfull.at[1, top], "hf2", at(pa, bl))

    scan_end("b", sc, gzc, b_prior, gb, gzb, True)

    def back_after(ci):
        rows = span(ci)
        grads = []
        for h, cols in enumerate(hcols):
            state = gb[ci, :, cols]
            gm[rows, cols] = gm[rows, cols] + nn(kf[rows, cols], state)
            grads.append(nt(u[rows, cols], state) + gzb[pl.ds(ci, 1), cols])
        gk = gks[rows] + feature_pull(k_ref[rows], jnp.concatenate(grads, axis=1))
        gk_t[:, rows] = gk.T.astype(BF16)

    loop(NC, back_after)
    send(gm.at[pl.ds(0, 8)], gm.at[pl.ds(TOK, 8)], "ghalo", earlier)
    results = []

    def give(src, dst):
        copy = pltpu.make_async_copy(src, dst, local_sems.at[9 + len(results)])
        copy.start()
        results.append(copy)

    give(gq_t, gq_hbm)
    give(gk_t, gk_hbm)

    arrived(hhalf.at[0], "hh0")
    hs[1, top] = (ph[br, top] + hhalf[0].astype(F32)).astype(BF16)
    send(hs.at[1, top], hfull.at[0, top], "hf0", at(pa, br))
    arrived(hhalf.at[1], "hh1")
    hs[2, bottom] = (ph[bl, bottom] + hhalf[1].astype(F32)).astype(BF16)
    send(hs.at[2, bottom], hfull.at[1, bottom], "hf3", at(pa, bl))

    arrived(gm.at[pl.ds(TOK, 8)], "ghalo")

    def tail(ci):
        rows = span(ci)
        here = gm[rows]
        after = gm[pl.ds(pl.multiple_of(ci * CH + CH, 8), 8)]
        after = jnp.where((ctx < 15) | (ci < NC - 1), after, 0.0)
        next1 = jnp.where(row_id == CH - 1, after[0:1], pltpu.roll(here, CH - 1, 0))
        next2 = jnp.where(
            row_id == CH - 1, after[1:2], jnp.where(row_id == CH - 2, after[0:1], pltpu.roll(here, CH - 2, 0))
        )
        total = cw_ref[0:1] * here + cw_ref[1:2] * next1 + cw_ref[2:3] * next2
        gab[rows] = total.astype(BF16)

    loop(NC, tail)
    give(gab, gv_hbm)

    for sources, rows in (((("of1", 0), ("of3", 1)), second), ((("of2", 1), ("of0", 0)), first)):
        for name, side in sources:
            arrived(rfull.at[side, rows], name)
        attp[rows] = (oo[rows] + rfull[0, rows].astype(F32) + rfull[1, rows].astype(F32)).astype(BF16)
        give(attp.at[rows], out_hbm.at[rows])

    for name, side, rows in (("hf1", 0, bottom), ("hf2", 1, top), ("hf0", 0, top), ("hf3", 1, bottom)):
        arrived(hfull.at[side, rows], name)
    total = ph[pb] + hfull[0].astype(F32) + hfull[1].astype(F32)
    gw_ref[...] = total.T
    give(gw_ref, gw_hbm)
    for copy in results:
        copy.wait()

    for copy in pending:
        copy.wait_send()


SEMS = 64


def settle(*refs):
    n = len(refs) // 3
    sources, targets, held, sems = refs[:n], refs[n : 2 * n], refs[2 * n : 3 * n], refs[3 * n]
    into = [pltpu.make_async_copy(a, b, sems.at[0, i]) for i, (a, b) in enumerate(zip(sources, held))]
    out = [pltpu.make_async_copy(a, b, sems.at[1, i]) for i, (a, b) in enumerate(zip(held, targets))]
    for copy in into:
        copy.start()
    for first, then in zip(into, out):
        first.wait()
        then.start()
    for copy in out:
        copy.wait()


def settled(arrays):
    hbm = pl.BlockSpec(memory_space=pl.ANY)
    shapes = [jax.ShapeDtypeStruct(a.shape, a.dtype) for a in arrays]
    return pl.pallas_call(
        settle,
        out_shape=tuple(shapes),
        in_specs=[hbm] * len(arrays),
        out_specs=(hbm,) * len(arrays),
        scratch_shapes=[pltpu.VMEM(a.shape, a.dtype) for a in arrays]
        + [pltpu.SemaphoreType.DMA((2, len(arrays)))],
        name="settle",
    )(*arrays)


def body(queries, keys, values, conv_weight, w_out, cotangent):
    first, second, rows = feature_tables()
    hbm = pl.BlockSpec(memory_space=pl.ANY)
    wide = HL * FEAT
    shapes = [
        ((wide, TOK), BF16), ((wide, TOK), BF16), ((3, COLS), F32), ((wide, HL * FW), BF16), ((wide, HL * FW), BF16),
        ((8, HL * FW), F32), ((TOK, wide), BF16), ((TOK, wide), BF16), ((wide, TOK), BF16), ((wide, TOK), BF16),
        ((256, COLS), F32),
        ((8, TOK, COLS), BF16), ((D, COLS), BF16), ((4, COLS, COLS), BF16), ((TOK + 16, COLS), BF16),
        ((TOK, COLS), BF16), ((TOK, HL * FW), BF16), ((TOK, HL * FW), BF16),
        ((TOK, COLS), F32), ((HL, TOK, 1), F32), ((HL, TOK, 1), F32),
        ((TOK, COLS), BF16), ((TOK, COLS), BF16), ((COLS, TOK), BF16),
        ((TOK, COLS), F32), ((TOK, COLS), BF16), ((TOK + 8, COLS), F32), ((TOK, HL * FEAT), F32),
        ((NC, FW, COLS), F32), ((NC, FW, COLS), BF16), ((NC, FW, COLS), BF16),
        ((8, HL * FW), F32), ((8, HL * FW), F32), ((8, HL * FW), F32), ((8, HL * FW), F32),
    ]
    for _ in range(2):
        shapes += [
            ((4, SR, 128), BF16), ((4, SR, 128), BF16), ((SR, 128), BF16),
            ((4, SR, 128), BF16), ((4, SR, 128), BF16), ((4, SR, 128), BF16),
        ]
    shapes += [
        ((3, TOK, COLS), BF16), ((TOK, COLS), F32), ((2, HALF, COLS), BF16), ((2, TOK, COLS), BF16),
        ((4, 4, COLS, 256), BF16), ((2, 2, COLS, 256), BF16), ((2, 4, COLS, 256), BF16),
        ((4, COLS, 256), F32), ((3, COLS, 256), BF16), ((2, 256, 256), BF16), ((2, COLS, 256), BF16),
    ]
    out, gq, gk, gv, gw = settled(pl.pallas_call(
        kernel,
        out_shape=(
            jax.ShapeDtypeStruct((TOK, COLS), BF16),
            jax.ShapeDtypeStruct((HL * FEAT, TOK), BF16),
            jax.ShapeDtypeStruct((HL * FEAT, TOK), BF16),
            jax.ShapeDtypeStruct((TOK, COLS), BF16),
            jax.ShapeDtypeStruct((256, COLS), F32),
        ),
        in_specs=[hbm] * 9,
        out_specs=(hbm,) * 5,
        scratch_shapes=[pltpu.VMEM(s, t) for s, t in shapes]
        + [pltpu.SemaphoreType.DMA((SEMS,)), pltpu.SemaphoreType.DMA((SEMS,)), pltpu.SemaphoreType.DMA((16,))],
        compiler_params=pltpu.CompilerParams(
            collective_id=0, has_side_effects=True, vmem_limit_bytes=67043328
        ),
        name="based_layer",
    )(
        queries.T, keys.T, conv_weight, jnp.asarray(first, BF16), jnp.asarray(second, BF16),
        jnp.asarray(rows, F32), values, w_out, cotangent,
    ))
    return out, gq.T, gk.T, gv, gw


def solution(mesh):
    split = P("ctx", "tp")
    return jax.shard_map(
        body,
        mesh=mesh,
        in_specs=(split, split, split, P(None, "tp"), P(None, "tp"), split),
        out_specs=(split,) * 5,
        check_vma=False,
    )
```

```python
import functools
import math

import jax
import jax.numpy as jnp
import numpy as np
from jax import lax
from jax.experimental import pallas as pl
from jax.experimental.pallas import tpu as pltpu
from jax.sharding import PartitionSpec as P

MESH = pl.DeviceIdType.MESH
F32 = jnp.float32
BF16 = jnp.bfloat16

FEAT = 16
HL = 2
DV = 256
COLS = HL * DV
TOK = 1024
D = 4096
CH = 256
NC = TOK // CH
HALF = TOK // 2
FW = 256
FR = 160
SR = FR + 16


def nn(a, b):
    return lax.dot_general(a, b, (((1,), (0,)), ((), ())), preferred_element_type=F32)


def nt(a, b):
    return lax.dot_general(a, b, (((1,), (1,)), ((), ())), preferred_element_type=F32)


def tn(a, b):
    return lax.dot_general(a, b, (((0,), (0,)), ((), ())), preferred_element_type=F32)


def feature_tables():
    pairs = [(FEAT, FEAT, 1.0)]
    pairs += [(i, FEAT, 1.0 / math.sqrt(math.sqrt(FEAT))) for i in range(FEAT)]
    for i in range(FEAT):
        for j in range(i, FEAT):
            scale = 1.0 / (math.sqrt(2.0) * math.sqrt(FEAT))
            pairs.append((i, j, scale if i == j else scale * math.sqrt(2.0)))
    first = np.zeros((HL * FEAT, HL * FW), np.float32)
    second = np.zeros((HL * FEAT, HL * FW), np.float32)
    rows = np.zeros((8, HL * FW), np.float32)
    for h in range(HL):
        for col, (i, j, scale) in enumerate(pairs):
            at = h * FW + col
            if i == FEAT:
                rows[0, at] = 1.0
            else:
                first[h * FEAT + i, at] = 1.0
            if j == FEAT:
                rows[1, at] = 1.0
            else:
                second[h * FEAT + j, at] = 1.0
            rows[2, at] = scale
    return first, second, rows


def kernel(
    q_hbm, k_hbm, cw_hbm, ra_hbm, rb_hbm, rows_hbm, val_hbm, w_hbm, cot_hbm,
    out_hbm, gq_hbm, gk_hbm, gv_hbm, gw_hbm,
    q_t, k_t, cw_ref, ra_ref, rb_ref, rows_ref, q_ref, k_ref, gq_t, gk_t, gw_ref,
    cfull, w, wx, vext, u, qf, kf, num, den, gd, att, attp, att_t, ga, gab, gm, gks,
    sc, sb, gb, zc, zb, gzc, gzb,
    f_send, f_line, f_tot, f_tots, f_back, f_prior,
    b_send, b_line, b_tot, b_tots, b_back, b_prior,
    so, oo, rhalf, rfull, gwt, ghalf, gfull, ph, hs, hhalf, hfull,
    send_sems, recv_sems, local_sems,
):
    ctx = lax.axis_index("ctx")
    tp = lax.axis_index("tp")
    x, z = ctx // 4, ctx % 4
    y, c = tp // 2, tp % 2
    yr, yl, yo = (y + 1) % 4, (y + 3) % 4, (y + 2) % 4
    partner = {"ctx": ctx, "tp": y * 2 + (1 - c)}
    to_right = {"ctx": ctx, "tp": yr * 2 + c}
    to_left = {"ctx": ctx, "tp": yl * 2 + c}
    later = {"ctx": (ctx + 1) % 16, "tp": tp}
    earlier = {"ctx": (ctx + 15) % 16, "tp": tp}
    zs = [{"ctx": x * 4 + (z + d) % 4, "tp": tp} for d in range(4)]
    xs = [{"ctx": ((x + d) % 4) * 4 + z, "tp": tp} for d in range(4)]

    names = {}
    pending = []

    def number(name):
        return names.setdefault(name, len(names))

    def remote(src, dst, name, dev):
        i = number(name)
        return pltpu.make_async_remote_copy(
            src_ref=src, dst_ref=dst, send_sem=send_sems.at[i], recv_sem=recv_sems.at[i],
            device_id=dev, device_id_type=MESH,
        )

    def send(src, dst, name, dev):
        copy = remote(src, dst, name, dev)
        copy.start()
        pending.append(copy)

    def arrived(dst, name):
        remote(dst, dst, name, partner).wait_recv()

    own_w = pltpu.make_async_copy(w_hbm, w, local_sems.at[0])
    own_v = pltpu.make_async_copy(val_hbm, vext.at[pl.ds(16, TOK)], local_sems.at[1])
    own_c = pltpu.make_async_copy(cot_hbm, cfull.at[tp], local_sems.at[2])
    own_v.start()
    small = [
        pltpu.make_async_copy(a, b, local_sems.at[3 + i])
        for i, (a, b) in enumerate((
            (q_hbm, q_t), (k_hbm, k_t), (cw_hbm, cw_ref), (ra_hbm, ra_ref), (rb_hbm, rb_ref), (rows_hbm, rows_ref),
        ))
    ]
    for copy in small:
        copy.start()
    own_c.start()
    own_w.start()

    barrier = pltpu.get_barrier_semaphore()
    peers = [partner, to_right, to_left, later, earlier] + zs[1:] + xs[1:]
    for peer in peers:
        pl.semaphore_signal(barrier, inc=1, device_id=peer, device_id_type=MESH)
    pl.semaphore_wait(barrier, len(peers))

    first, second = pl.ds(0, HALF), pl.ds(HALF, HALF)
    mine, from_r, from_l, from_o = tp, yr * 2 + c, yl * 2 + c, yo * 2 + c
    send(val_hbm.at[pl.ds(TOK - 16, 16)], vext.at[pl.ds(0, 16)], "halo", later)
    send(cot_hbm.at[first], cfull.at[mine, first], "r0", to_right)
    send(cot_hbm.at[second], cfull.at[mine, second], "l1", to_left)
    send(cot_hbm.at[second], cfull.at[mine, second], "r1", to_right)
    send(cot_hbm.at[first], cfull.at[mine, first], "l0", to_left)
    send(cot_hbm, cfull.at[mine], "p", partner)
    for yy in range(4):
        rows = pl.ds(pl.multiple_of((yy * 2 + 1 - c) * COLS, COLS), COLS)
        send(w_hbm.at[rows], wx.at[yy], ("w", yy), partner)

    def span(i, size=CH):
        return pl.ds(pl.multiple_of(i * size, size), size)

    lane = lax.broadcasted_iota(jnp.int32, (CH, HL * FEAT), 1)
    row_id = lax.broadcasted_iota(jnp.int32, (CH, COLS), 0)
    causal = lax.broadcasted_iota(jnp.int32, (CH, CH), 0) >= lax.broadcasted_iota(jnp.int32, (CH, CH), 1)

    def head_of(value, h):
        return jnp.where(lane // FEAT == h, value, jnp.zeros_like(value))

    def factors(value):
        return nn(value, ra_ref[...]) + rows_ref[0:1], nn(value, rb_ref[...]) + rows_ref[1:2]

    def features(value):
        a, b = factors(value)
        return (a * b * rows_ref[2:3]).astype(BF16)

    def feature_pull(value, grad):
        a, b = factors(value)
        scaled = grad * rows_ref[2:3]
        return nt((scaled * b).astype(BF16), ra_ref[...]) + nt((scaled * a).astype(BF16), rb_ref[...])

    def loop(n, body):
        def step(i, carry):
            body(i)
            return carry

        lax.fori_loop(0, n, step, 0)

    hcols = [slice(h * DV, (h + 1) * DV) for h in range(HL)]

    for copy in small:
        copy.wait()
    own_v.wait()
    arrived(vext.at[pl.ds(0, 16)], "halo")

    def front(ci):
        rows = span(ci)
        before = vext[pl.ds(pl.multiple_of(ci * CH, CH), 16)].astype(F32)
        before = jnp.where((ctx > 0) | (ci > 0), before, 0.0)
        here = vext[pl.ds(pl.multiple_of(ci * CH + 16, 16), CH)].astype(F32)
        back1 = jnp.where(row_id == 0, before[15:16], pltpu.roll(here, 1, 0))
        back2 = jnp.where(
            row_id == 0, before[14:15], jnp.where(row_id == 1, before[15:16], pltpu.roll(here, 2, 0))
        )
        mixed = cw_ref[0:1] * here + cw_ref[1:2] * back1 + cw_ref[2:3] * back2
        mixed = mixed.astype(BF16)
        u[rows] = mixed
        qq, kk = q_t[:, rows].T, k_t[:, rows].T
        q_ref[rows], k_ref[rows] = qq, kk
        qf[rows] = features(qq)
        kk = features(kk)
        kf[rows] = kk
        for cols in hcols:
            sc[ci, :, cols] = tn(kk[:, cols], mixed[:, cols])
        zc[pl.ds(ci, 1)] = jnp.sum(kk.astype(F32), axis=0, keepdims=True)

    loop(NC, front)

    def scan_open(tag, states, norms, s_send, s_line):
        for j in range(4):
            cols = slice(j * 128, (j + 1) * 128)
            total = states[0, 0:FR, cols]
            for ci in range(1, NC):
                total = total + states[ci, 0:FR, cols]
            norm = jnp.sum(norms[0:NC, cols], axis=0, keepdims=True)
            s_send[j, 0:FR] = total.astype(BF16)
            s_send[j, FR:SR] = jnp.broadcast_to(norm, (16, 128)).astype(BF16)
        for d in range(1, 4):
            send(s_send.at[(z + d) % 4], s_line.at[z], (tag, 1, d), zs[d])
        s_line[z] = s_send[z]

    def scan_middle(tag, s_line, s_tot, s_tots):
        for d in range(1, 4):
            arrived(s_line.at[(z + 4 - d) % 4], (tag, 1, d))
        total = s_line[0].astype(F32)
        for i in range(1, 4):
            total = total + s_line[i].astype(F32)
        s_tot[...] = total.astype(BF16)
        for d in range(1, 4):
            send(s_tot, s_tots.at[x], (tag, 2, d), xs[d])

    def scan_close(tag, s_line, s_tots, s_back, s_prior, backward):
        for d in range(1, 4):
            arrived(s_tots.at[(x + 4 - d) % 4], (tag, 2, d))
        run = jnp.zeros((SR, 128), F32)
        for i in range(4):
            wanted = (i > x) if backward else (i < x)
            run = run + jnp.where(wanted, s_tots[i].astype(F32), 0.0)
        for i in reversed(range(4)) if backward else range(4):
            s_back[i] = run.astype(BF16)
            run = run + s_line[i].astype(F32)
        for d in range(1, 4):
            send(s_back.at[(z + d) % 4], s_prior.at[z], (tag, 3, d), zs[d])
        s_prior[z] = s_back[z]

    def scan_end(tag, states, norms, s_prior, to_states, to_norms, backward):
        for d in range(1, 4):
            arrived(s_prior.at[(z + 4 - d) % 4], (tag, 3, d))
        for j in range(4):
            cols = slice(j * 128, (j + 1) * 128)
            run = s_prior[j, 0:FR].astype(F32)
            norm = s_prior[j, FR:SR].astype(F32)[0:1]
            for ci in reversed(range(NC)) if backward else range(NC):
                to_states[ci, 0:FR, cols] = run.astype(BF16)
                to_states[ci, FR:FW, cols] = jnp.zeros((FW - FR, 128), BF16)
                to_norms[ci : ci + 1, cols] = norm
                run = run + states[ci, 0:FR, cols]
                norm = norm + norms[ci : ci + 1, cols]

    scan_open("f", sc, zc, f_send, f_line)

    def scores_of(ci, h):
        s = nt(head_of(q_ref[span(ci)], h), k_ref[span(ci)]) * (1.0 / math.sqrt(FEAT))
        return s, jnp.where(causal, 1.0 + s + 0.5 * s * s, 0.0)

    def inside(ci):
        rows = span(ci)
        for h, cols in enumerate(hcols):
            _, weight = scores_of(ci, h)
            num[rows, cols] = nn(weight.astype(BF16), u[rows, cols])
            den[h, rows] = jnp.sum(weight, axis=1, keepdims=True)

    loop(NC, inside)
    scan_middle("f", f_line, f_tot, f_tots)

    def pull(block, start=False):
        wrows = pl.ds(pl.multiple_of(block * COLS, COLS), COLS)

        def part(r):
            rows = span(r, HALF)
            got = nn(cfull[block, rows], w[wrows])
            ga[rows] = got if start else ga[rows] + got

        loop(2, part)

    own_c.wait()
    own_w.wait()
    pull(mine, True)

    arrived(cfull.at[from_l, first], "r0")
    send(cfull.at[from_l, first], cfull.at[from_l, first], "fr", to_right)
    send(cfull.at[from_l, first], cfull.at[from_l, first], "pl0", partner)
    arrived(cfull.at[from_r, second], "l1")
    send(cfull.at[from_r, second], cfull.at[from_r, second], "fl", to_left)
    send(cfull.at[from_r, second], cfull.at[from_r, second], "pr1", partner)

    scan_close("f", f_line, f_tots, f_back, f_prior, False)
    other = y * 2 + 1 - c
    arrived(cfull.at[other], "p")
    pull(other)

    scan_end("f", sc, zc, f_prior, sb, zb, False)

    def finish(ci):
        rows = span(ci)
        pieces = []
        for h, cols in enumerate(hcols):
            qh = qf[rows, cols]
            n = num[rows, cols] + nn(qh, sb[ci, :, cols])
            below = den[h, rows] + jnp.sum(qh.astype(F32) * zb[pl.ds(ci, 1), cols], axis=1, keepdims=True)
            r = 1.0 / below
            num[rows, cols] = n
            den[h, rows] = r
            pieces.append((n * r).astype(BF16))
            att[rows, cols] = pieces[-1]
        for h in range(HL):
            att_t[h * DV : (h + 1) * DV, rows] = pieces[h].T

    loop(NC, finish)
    send(att, attp, "att", partner)

    arrived(cfull.at[from_l, second], "r1")
    send(cfull.at[from_l, second], cfull.at[from_l, second], "pl1", partner)
    arrived(cfull.at[from_r, first], "l0")
    send(cfull.at[from_r, first], cfull.at[from_r, first], "pr0", partner)
    pull(from_l)

    for yy in range(4):
        arrived(wx.at[yy], ("w", yy))
    arrived(attp, "att")

    def project(yy, r):
        rows = pl.ds(r * HALF, HALF)
        wrows = pl.ds(pl.multiple_of((yy * 2 + c) * COLS, COLS), COLS)
        return nt(att[rows], w[wrows]) + nt(attp[rows], wx[yy])

    so[0, first] = project(yo, 0).astype(BF16)
    send(so.at[0, first], rhalf.at[0], "oh0", to_right)
    so[0, second] = project(yo, 1).astype(BF16)
    send(so.at[0, second], rhalf.at[1], "oh1", to_left)
    so[1, second] = project(yr, 1).astype(BF16)
    send(so.at[1, second], rfull.at[0, second], "of1", to_right)
    so[2, first] = project(yl, 0).astype(BF16)
    send(so.at[2, first], rfull.at[1, first], "of2", to_left)

    along_x = c == 0
    pa = jnp.where(along_x, x, z)
    pb = jnp.where(along_x, z, x)

    def at(a, b):
        return {"ctx": jnp.where(along_x, a * 4 + b, b * 4 + a), "tp": tp}

    ar, al, ao = (pa + 1) % 4, (pa + 3) % 4, (pa + 2) % 4
    br, bl, bo = (pb + 1) % 4, (pb + 3) % 4, (pb + 2) % 4

    def tiles(block):
        for half in range(2):
            i = 2 * block + half
            a, b = jnp.where(along_x, i // 4, i % 4), jnp.where(along_x, i % 4, i // 4)
            gwt[a, b] = nn(att_t[...], cfull[block, :, half * 256 : half * 256 + 256]).astype(BF16)

    p_l, p_r, p_o = yl * 2 + 1 - c, yr * 2 + 1 - c, yo * 2 + 1 - c
    pull(from_r)

    def ready(n):
        tiles(jnp.where(n == 0, mine, jnp.where(n == 1, other, jnp.where(n == 2, from_l, from_r))))

    loop(4, ready)
    arrived(cfull.at[p_l, first], "pl0")
    arrived(cfull.at[p_l, second], "pl1")
    pull(p_l)
    arrived(cfull.at[p_r, first], "pr0")
    arrived(cfull.at[p_r, second], "pr1")
    pull(p_r)

    def ready_too(n):
        tiles(jnp.where(n == 0, p_l, p_r))

    loop(2, ready_too)
    low, high = pl.ds(0, 2), pl.ds(2, 2)

    def known(group, upper):
        return jnp.where(along_x, group != yo, (yo < 2) if upper else (yo >= 2))

    gw_first = [
        (known(ao, False), gwt.at[ao, low], ghalf.at[0], "gh0", at(ar, pb)),
        (known(ao, True), gwt.at[ao, high], ghalf.at[1], "gh1", at(al, pb)),
        (known(ar, True), gwt.at[ar, high], gfull.at[0, high], "gf1", at(ar, pb)),
        (known(al, False), gwt.at[al, low], gfull.at[1, low], "gf2", at(al, pb)),
    ]

    def send_if(when, src, dst, name, dev):
        @pl.when(when)
        def _():
            remote(src, dst, name, dev).start()

    for when, *rest in gw_first[:4]:
        send_if(when, *rest)
    arrived(cfull.at[from_o, first], "fr")
    send(cfull.at[from_o, first], cfull.at[from_o, first], "po0", partner)
    arrived(cfull.at[from_o, second], "fl")
    send(cfull.at[from_o, second], cfull.at[from_o, second], "po1", partner)
    tiles(from_o)
    pull(from_o)
    arrived(cfull.at[p_o, first], "po0")
    arrived(cfull.at[p_o, second], "po1")
    tiles(p_o)
    for when, *rest in gw_first[:4]:
        send_if(jnp.logical_not(when), *rest)
        pending.append(remote(*rest))
    pull(p_o)

    def back_states(ci):
        rows = span(ci)
        for h, cols in enumerate(hcols):
            g = ga[rows, cols].astype(BF16)
            gab[rows, cols] = g
            r = den[h, rows]
            dd = -jnp.sum(g.astype(F32) * num[rows, cols], axis=1, keepdims=True) * r * r
            gd[h, rows] = dd
            qh = qf[rows, cols].astype(F32)
            sc[ci, :, cols] = tn((qh * r).astype(BF16), g)
            gzc[pl.ds(ci, 1), cols] = jnp.sum(qh * dd, axis=0, keepdims=True)

    loop(NC, back_states)
    scan_open("b", sc, gzc, b_send, b_line)
    so[1, first] = project(yr, 0).astype(BF16)
    so[2, second] = project(yl, 1).astype(BF16)

    def back_inside(ci):
        rows = span(ci)
        gq = jnp.zeros((CH, HL * FEAT), F32)
        gk = jnp.zeros((CH, HL * FEAT), F32)
        grads = []
        for h, cols in enumerate(hcols):
            s, weight = scores_of(ci, h)
            r, dd, g = den[h, rows], gd[h, rows], gab[rows, cols]
            m = nt(g, u[rows, cols]) * r + dd
            m = jnp.where(causal, m * (1.0 + s) * (1.0 / math.sqrt(FEAT)), 0.0).astype(BF16)
            gq = gq + nn(m, head_of(k_ref[rows], h))
            gk = gk + tn(m, head_of(q_ref[rows], h))
            gm[rows, cols] = tn((weight * r).astype(BF16), g)
            grads.append(nt(g, sb[ci, :, cols]) * r + dd * zb[pl.ds(ci, 1), cols])
        gks[rows] = gk
        gq = gq + feature_pull(q_ref[rows], jnp.concatenate(grads, axis=1))
        gq_t[:, rows] = gq.T.astype(BF16)

    loop(1, back_inside)
    scan_middle("b", b_line, b_tot, b_tots)

    arrived(rhalf.at[0], "oh0")
    so[1, first] = (so[1, first].astype(F32) + rhalf[0].astype(F32)).astype(BF16)
    send(so.at[1, first], rfull.at[0, first], "of0", to_right)
    arrived(rhalf.at[1], "oh1")
    so[2, second] = (so[2, second].astype(F32) + rhalf[1].astype(F32)).astype(BF16)
    send(so.at[2, second], rfull.at[1, second], "of3", to_left)

    def back_inside_rest(n):
        back_inside(n + 1)

    loop(1, back_inside_rest)
    arrived(ghalf.at[0], "gh0")
    arrived(ghalf.at[1], "gh1")

    def joined(b):
        gwt[ar, b] = (gwt[ar, b].astype(F32) + ghalf[0, b].astype(F32)).astype(BF16)
        gwt[al, b + 2] = (gwt[al, b + 2].astype(F32) + ghalf[1, b].astype(F32)).astype(BF16)

    loop(2, joined)
    send(gwt.at[ar, low], gfull.at[0, low], "gf0", at(ar, pb))
    send(gwt.at[al, high], gfull.at[1, high], "gf3", at(al, pb))
    scan_close("b", b_line, b_tots, b_back, b_prior, True)

    def back_inside_last(n):
        back_inside(n + 2)

    loop(2, back_inside_last)


    arrived(gfull.at[0, high], "gf1")
    arrived(gfull.at[1, low], "gf2")
    arrived(gfull.at[0, low], "gf0")
    arrived(gfull.at[1, high], "gf3")

    def own_sum(b):
        ph[b] = gwt[pa, b].astype(F32) + gfull[0, b].astype(F32) + gfull[1, b].astype(F32)

    loop(4, own_sum)
    top, bottom = pl.ds(0, 256), pl.ds(256, 256)
    hs[0] = ph[bo].astype(BF16)
    send(hs.at[0, top], hhalf.at[0], "hh0", at(pa, br))
    send(hs.at[0, bottom], hhalf.at[1], "hh1", at(pa, bl))
    hs[1, bottom] = ph[br, bottom].astype(BF16)
    send(hs.at[1, bottom], hfull.at[0, bottom], "hf1", at(pa, br))
    hs[2, top] = ph[bl, top].astype(BF16)
    send(hs.at[2, top], hfull.at[1, top], "hf2", at(pa, bl))

    def own_out(r):
        rows = span(r, HALF)
        wrows = pl.ds(pl.multiple_of((y * 2 + c) * COLS, COLS), COLS)
        oo[rows] = nt(att[rows], w[wrows]) + nt(attp[rows], wx[y])

    loop(2, own_out)

    scan_end("b", sc, gzc, b_prior, gb, gzb, True)

    def back_after(ci):
        rows = span(ci)
        grads = []
        for h, cols in enumerate(hcols):
            state = gb[ci, :, cols]
            gm[rows, cols] = gm[rows, cols] + nn(kf[rows, cols], state)
            grads.append(nt(u[rows, cols], state) + gzb[pl.ds(ci, 1), cols])
        gk = gks[rows] + feature_pull(k_ref[rows], jnp.concatenate(grads, axis=1))
        gk_t[:, rows] = gk.T.astype(BF16)

    loop(NC, back_after)
    send(gm.at[pl.ds(0, 8)], gm.at[pl.ds(TOK, 8)], "ghalo", earlier)
    results = []

    def give(src, dst):
        copy = pltpu.make_async_copy(src, dst, local_sems.at[9 + len(results)])
        copy.start()
        results.append(copy)

    give(gq_t, gq_hbm)
    give(gk_t, gk_hbm)

    arrived(hhalf.at[0], "hh0")
    hs[1, top] = (ph[br, top] + hhalf[0].astype(F32)).astype(BF16)
    send(hs.at[1, top], hfull.at[0, top], "hf0", at(pa, br))
    arrived(hhalf.at[1], "hh1")
    hs[2, bottom] = (ph[bl, bottom] + hhalf[1].astype(F32)).astype(BF16)
    send(hs.at[2, bottom], hfull.at[1, bottom], "hf3", at(pa, bl))

    arrived(gm.at[pl.ds(TOK, 8)], "ghalo")

    def tail(ci):
        rows = span(ci)
        here = gm[rows]
        after = gm[pl.ds(pl.multiple_of(ci * CH + CH, 8), 8)]
        after = jnp.where((ctx < 15) | (ci < NC - 1), after, 0.0)
        next1 = jnp.where(row_id == CH - 1, after[0:1], pltpu.roll(here, CH - 1, 0))
        next2 = jnp.where(
            row_id == CH - 1, after[1:2], jnp.where(row_id == CH - 2, after[0:1], pltpu.roll(here, CH - 2, 0))
        )
        total = cw_ref[0:1] * here + cw_ref[1:2] * next1 + cw_ref[2:3] * next2
        gab[rows] = total.astype(BF16)

    loop(NC, tail)
    give(gab, gv_hbm)

    for sources, rows in (((("of1", 0), ("of3", 1)), second), ((("of2", 1), ("of0", 0)), first)):
        for name, side in sources:
            arrived(rfull.at[side, rows], name)
        attp[rows] = (oo[rows] + rfull[0, rows].astype(F32) + rfull[1, rows].astype(F32)).astype(BF16)
        give(attp.at[rows], out_hbm.at[rows])

    for name, side, rows in (("hf1", 0, bottom), ("hf2", 1, top), ("hf0", 0, top), ("hf3", 1, bottom)):
        arrived(hfull.at[side, rows], name)
    total = ph[pb] + hfull[0].astype(F32) + hfull[1].astype(F32)
    gw_ref[...] = total.T
    give(gw_ref, gw_hbm)
    for copy in results:
        copy.wait()

    for copy in pending:
        copy.wait_send()


SEMS = 64


def settle(*refs):
    n = len(refs) // 3
    sources, targets, held, sems = refs[:n], refs[n : 2 * n], refs[2 * n : 3 * n], refs[3 * n]
    into = [pltpu.make_async_copy(a, b, sems.at[0, i]) for i, (a, b) in enumerate(zip(sources, held))]
    out = [pltpu.make_async_copy(a, b, sems.at[1, i]) for i, (a, b) in enumerate(zip(held, targets))]
    for copy in into:
        copy.start()
    for first, then in zip(into, out):
        first.wait()
        then.start()
    for copy in out:
        copy.wait()


def settled(arrays):
    hbm = pl.BlockSpec(memory_space=pl.ANY)
    shapes = [jax.ShapeDtypeStruct(a.shape, a.dtype) for a in arrays]
    return pl.pallas_call(
        settle,
        out_shape=tuple(shapes),
        in_specs=[hbm] * len(arrays),
        out_specs=(hbm,) * len(arrays),
        scratch_shapes=[pltpu.VMEM(a.shape, a.dtype) for a in arrays]
        + [pltpu.SemaphoreType.DMA((2, len(arrays)))],
        name="settle",
    )(*arrays)


def body(queries, keys, values, conv_weight, w_out, cotangent):
    first, second, rows = feature_tables()
    hbm = pl.BlockSpec(memory_space=pl.ANY)
    wide = HL * FEAT
    shapes = [
        ((wide, TOK), BF16), ((wide, TOK), BF16), ((3, COLS), F32), ((wide, HL * FW), BF16), ((wide, HL * FW), BF16),
        ((8, HL * FW), F32), ((TOK, wide), BF16), ((TOK, wide), BF16), ((wide, TOK), BF16), ((wide, TOK), BF16),
        ((256, COLS), F32),
        ((8, TOK, COLS), BF16), ((D, COLS), BF16), ((4, COLS, COLS), BF16), ((TOK + 16, COLS), BF16),
        ((TOK, COLS), BF16), ((TOK, HL * FW), BF16), ((TOK, HL * FW), BF16),
        ((TOK, COLS), F32), ((HL, TOK, 1), F32), ((HL, TOK, 1), F32),
        ((TOK, COLS), BF16), ((TOK, COLS), BF16), ((COLS, TOK), BF16),
        ((TOK, COLS), F32), ((TOK, COLS), BF16), ((TOK + 8, COLS), F32), ((TOK, HL * FEAT), F32),
        ((NC, FW, COLS), F32), ((NC, FW, COLS), BF16), ((NC, FW, COLS), BF16),
        ((8, HL * FW), F32), ((8, HL * FW), F32), ((8, HL * FW), F32), ((8, HL * FW), F32),
    ]
    for _ in range(2):
        shapes += [
            ((4, SR, 128), BF16), ((4, SR, 128), BF16), ((SR, 128), BF16),
            ((4, SR, 128), BF16), ((4, SR, 128), BF16), ((4, SR, 128), BF16),
        ]
    shapes += [
        ((3, TOK, COLS), BF16), ((TOK, COLS), F32), ((2, HALF, COLS), BF16), ((2, TOK, COLS), BF16),
        ((4, 4, COLS, 256), BF16), ((2, 2, COLS, 256), BF16), ((2, 4, COLS, 256), BF16),
        ((4, COLS, 256), F32), ((3, COLS, 256), BF16), ((2, 256, 256), BF16), ((2, COLS, 256), BF16),
    ]
    out, gq, gk, gv, gw = settled(pl.pallas_call(
        kernel,
        out_shape=(
            jax.ShapeDtypeStruct((TOK, COLS), BF16),
            jax.ShapeDtypeStruct((HL * FEAT, TOK), BF16),
            jax.ShapeDtypeStruct((HL * FEAT, TOK), BF16),
            jax.ShapeDtypeStruct((TOK, COLS), BF16),
            jax.ShapeDtypeStruct((256, COLS), F32),
        ),
        in_specs=[hbm] * 9,
        out_specs=(hbm,) * 5,
        scratch_shapes=[pltpu.VMEM(s, t) for s, t in shapes]
        + [pltpu.SemaphoreType.DMA((SEMS,)), pltpu.SemaphoreType.DMA((SEMS,)), pltpu.SemaphoreType.DMA((16,))],
        compiler_params=pltpu.CompilerParams(
            collective_id=0, has_side_effects=True, vmem_limit_bytes=67043328
        ),
        name="based_layer",
    )(
        queries.T, keys.T, conv_weight, jnp.asarray(first, BF16), jnp.asarray(second, BF16),
        jnp.asarray(rows, F32), values, w_out, cotangent,
    ))
    return out, gq.T, gk.T, gv, gw


def solution(mesh):
    split = P("ctx", "tp")
    return jax.shard_map(
        body,
        mesh=mesh,
        in_specs=(split, split, split, P(None, "tp"), P(None, "tp"), split),
        out_specs=(split,) * 5,
        check_vma=False,
    )
```
